512 devices in a mesh: depth: 32 (over y_hi, z), src: 16 (over x, y_lo, core).
Axes of the slice: x: 4, y: 4 (y_hi: 2, y_lo: 2; y = y_hi * 2 + y_lo), z: 16, core: 2. Of those that a mesh axis runs over, the one named last changes fastest.
Arguments:
- forward: bfloat16 [32, 128, 128, 128], P('src', 'depth'), may hold values from 0.099609375 to 3
- detectors: int32 [524288], P('depth'), may hold values from 0 to 65535, as said below
- residuals: float32 [32, 524288], P('src', 'depth'), may hold values from -6 to 6
- delay_index: int32 [32], P('src'), may hold values from 0 to 7
- labels: int32 [128, 128, 128], P('depth'), may hold values from 0 to 4
- blood_flow: float32 [128, 128, 128], P('depth'), may hold values from 0.2 to 5
- diff_table: float32 [5], replicated, may hold values from 0.5 to 1.5
- absorb_table: float32 [5], replicated, may hold values from 0.05 to 0.5
- delay_tau: float32 [8], replicated, may hold values from 0.1 to 1
- delay_weight: float32 [8], replicated, may hold values from 0.5 to 2
Outputs:
- gradient: float32 [128, 128, 128], P('depth', 'src')
The draws below stay inside these ranges and needn't reach their ends.
Inputs may be any that keep to these rules, and one draw needn't show every extreme that they name: `detectors`: detectors 16384 * j to 16384 * (j + 1) - 1 belong to the depth slab of planes 4 * j to 4 * (j + 1) - 1, and each holds a flat index within that slab (z - 4 * j) * 128 * 128 + y * 128 + x; the first of each such block is 0 and the last is 65535; voxels may repeat.
All inputs are finite; a program needn't handle non-finite values.
Results may differ from the reference program's by a relative error of at most 0.00035.
Values sent between devices are 32-bit elements; how exact they have to be, the bound alone decides.
A program may use at most 128 MiB of HBM per device.

```python
import math
import jax
import jax.numpy as jnp
from jax import lax

CZ = 4
NY = 128
NX = 128
DET_DEV = 16384
NLABEL = 5
NDELAY = 8
CHEB = 3
NZ = 128
PAIRS = 32
NDET = 524288


def draw_detectors(key, part):
    slab_cells = CZ * NY * NX
    slabs = NZ // CZ
    local_index = jax.random.randint(key, (slabs, DET_DEV), 0, slab_cells)
    local_index = local_index.at[:, 0].set(0)
    local_index = local_index.at[:, DET_DEV - 1].set(slab_cells - 1)
    return local_index.reshape(-1).astype(jnp.int32)


def set_ends(values, own_key, smallest, largest):
    longest = values.shape.index(max(values.shape))
    spots = []
    for shift in (0, 1):
        where = [jax.random.randint(jax.random.fold_in(own_key, axis), (), 0, length) for axis, length in enumerate(values.shape)]
        where[longest] = (where[longest] + shift) % values.shape[longest]
        spots.append(tuple(where))
    return values.at[spots[0]].set(smallest).at[spots[1]].set(largest)


def levels(rng, shape, split, smallest, largest):
    def one(axis_at, parts):
        draws = jax.random.uniform(jax.random.fold_in(jax.random.fold_in(rng, 6), axis_at), (parts,), jnp.float32, smallest / len(split), largest / len(split))
        return jnp.repeat(jnp.exp(draws), shape[axis_at] // parts).reshape((-1,) + (1,) * (len(shape) - axis_at - 1))

    loudness = one(*split[0])
    for cut in split[1:]:
        loudness = loudness * one(*cut)
    return loudness


def bell_draw(stream_key, dims, deviation, reach, pieces=(), kind=jnp.bfloat16):
    entries = jax.random.normal(stream_key, dims, jnp.float32) * deviation
    if len(pieces) > 0:
        entries = levels(stream_key, dims, pieces, -0.22, 0.18) * entries
    return jnp.clip(entries, min=-reach, max=reach).astype(kind)


def setup_inputs(seed: int = 0) -> dict:
    key_of = jax.random.split(jax.random.key(seed), 11)
    return {
        "forward": jnp.clip(jnp.exp(math.log(3.0) - 3.4051113 * jax.random.uniform(key_of[0], (PAIRS, NZ, NY, NX), jnp.float32) ** levels(key_of[0], (PAIRS, NZ, NY, NX), ((0, 16), (1, 32)), -0.2, 0.2)), 0.099609375, 3.0).astype(jnp.bfloat16),
        "detectors": draw_detectors(jax.random.fold_in(key_of[10], 71), 0),
        "residuals": bell_draw(key_of[2], (PAIRS, NDET), 1.0, 6.0, ((0, 16), (1, 32)), jnp.float32),
        "delay_index": set_ends(jax.random.randint(key_of[3], (PAIRS,), 0, NDELAY), jax.random.fold_in(key_of[3], 1), 0, NDELAY - 1).astype(jnp.int32),
        "labels": set_ends(jax.random.randint(key_of[4], (NZ, NY, NX), 0, NLABEL), jax.random.fold_in(key_of[4], 1), 0, NLABEL - 1).astype(jnp.int32),
        "blood_flow": jnp.clip(jnp.exp(math.log(5.0) - 3.218876 * jax.random.uniform(key_of[5], (NZ, NY, NX), jnp.float32) ** levels(key_of[5], (NZ, NY, NX), ((0, 32),), -0.2, 0.2)), 0.2, 5.0),
        "diff_table": jnp.clip(jax.random.uniform(key_of[6], (NLABEL,), jnp.float32, 0.5, 1.5), 0.5, 1.5),
        "absorb_table": jnp.clip(jax.random.uniform(key_of[7], (NLABEL,), jnp.float32, 0.05, 0.5), 0.05, 0.5),
        "delay_tau": jnp.clip(jnp.exp(jax.random.uniform(key_of[8], (NDELAY,), jnp.float32, math.log(0.1), math.log(1.0))), 0.1, 1.0),
        "delay_weight": jnp.clip(jnp.exp(jax.random.uniform(key_of[9], (NDELAY,), jnp.float32, math.log(0.5), math.log(2.0))), 0.5, 2.0),
    }


SPECTRUM_LOW = 0.1
SPECTRUM_HIGH = 2.0


def lookup(values_table, label_keys):
    result = jnp.zeros(label_keys.shape, jnp.float32)
    for entry in range(values_table.shape[0]):
        result = result + jnp.where(label_keys == entry, values_table[entry], jnp.float32(0.0))
    return result


def neighbor(array, which_axis, offset):
    window = [slice(1, array.shape[array.ndim - 3 + spatial] - 1) for spatial in range(3)]
    extent = array.shape[array.ndim - 3 + which_axis]
    window[which_axis] = slice(offset, extent - 2 + offset)
    leading = tuple(slice(None) for leading_dim in range(array.ndim - 3))
    return array[leading + tuple(window)]


def operate(field_pad, diffusion_pad, absorb):
    centre_field = neighbor(field_pad, 0, 1)
    centre_diff = neighbor(diffusion_pad, 0, 1)
    result = absorb * centre_field
    for which_axis in range(3):
        for offset in (0, 2):
            face_coef = 0.5 * (centre_diff + neighbor(diffusion_pad, which_axis, offset))
            result = result + face_coef * (centre_field - neighbor(field_pad, which_axis, offset))
    return result


def diagonal(diffusion_pad, absorb):
    centre_diff = neighbor(diffusion_pad, 0, 1)
    result = absorb
    for which_axis in range(3):
        for offset in (0, 2):
            result = result + 0.5 * (centre_diff + neighbor(diffusion_pad, which_axis, offset))
    return result


def chebyshev(source_term, diagonal_terms, apply_fn, keep_fn):
    centre = 0.5 * (SPECTRUM_HIGH + SPECTRUM_LOW)
    half_width = 0.5 * (SPECTRUM_HIGH - SPECTRUM_LOW)
    ratio_sigma = centre / half_width
    rho_prev = 1.0 / ratio_sigma
    step_field = keep_fn(source_term / diagonal_terms / centre)
    iterate = step_field
    residual = source_term
    for turn in range(1, CHEB):
        residual = residual - apply_fn(step_field)
        rho_now = 1.0 / (2.0 * ratio_sigma - rho_prev)
        step_field = keep_fn(rho_now * rho_prev * step_field + (2.0 * rho_now / half_width) * (residual / diagonal_terms))
        iterate = iterate + step_field
        rho_prev = rho_now
    return iterate


def identity_keep(step_field):
    return step_field


def reference(forward, detectors, residuals, delay_index, labels, blood_flow, diff_table, absorb_table, delay_tau, delay_weight):
    diffusion = lookup(diff_table, labels)
    base_absorb = lookup(absorb_table, labels)
    diffusion_pad = jnp.pad(diffusion, 1)
    pair_tau = lookup(delay_tau, delay_index)
    pair_weight = lookup(delay_weight, delay_index)
    slab_number = (jnp.arange(NDET, dtype=jnp.int32) // DET_DEV).astype(jnp.int32)
    flat_index = (detectors + slab_number * (CZ * NY * NX)).astype(jnp.int32)

    def one_pair(gradient_sum, pair_items):
        forward_field, residual_row, tau_value, weight_value = pair_items
        absorb = base_absorb + tau_value * blood_flow
        diagonal_terms = diagonal(diffusion_pad, absorb)
        source_term = jnp.zeros((NZ * NY * NX,), jnp.float32).at[flat_index].add(residual_row).reshape(NZ, NY, NX)

        def apply_fn(step_field):
            return operate(jnp.pad(step_field, 1), diffusion_pad, absorb)

        adjoint = chebyshev(source_term, diagonal_terms, apply_fn, identity_keep)
        pair_coef = -(weight_value * tau_value)
        return gradient_sum + pair_coef * forward_field.astype(jnp.float32) * adjoint, None

    start = jnp.zeros((NZ, NY, NX), jnp.float32)
    gradient_sum, unused = lax.scan(one_pair, start, (forward, residuals, pair_tau, pair_weight))
    return gradient_sum
```

```python
import functools

import jax
import jax.numpy as jnp
from jax import lax
from jax.experimental import pallas as pl
from jax.experimental.pallas import tpu as pltpu
from jax.sharding import PartitionSpec as P

SPECTRUM_LOW = 0.1
SPECTRUM_HIGH = 2.0
CENTRE = 0.5 * (SPECTRUM_HIGH + SPECTRUM_LOW)
HALF = 0.5 * (SPECTRUM_HIGH - SPECTRUM_LOW)
SIGMA = CENTRE / HALF
RHO0 = 1.0 / SIGMA
RHO1 = 1.0 / (2.0 * SIGMA - RHO0)
RHO2 = 1.0 / (2.0 * SIGMA - RHO1)

N = 128
CHUNK = 1024
MESH = pl.DeviceIdType.MESH
F32 = jnp.float32
BF16 = jnp.bfloat16


def lookup(table, labels, count):
    value = jnp.zeros(labels.shape, F32)
    for entry in range(count):
        value = jnp.where(labels == entry, table[entry], value)
    return value


def kernel(
    groups, depths,
    fwd, det, res, labels, flow, index, dtab, atab, tau, wgt,
    out,
    rt, acc, lab_h, diff, inv, gx, gy, gz, d0, d1, q1, d0h, d1h, part, recv,
    lab_s, lab_r, d0_s, d0_r, d1_s, d1_r, rs_s, rs_r,
):
    me = lax.axis_index("src")
    z = lax.axis_index("depth")
    up = lax.rem(z + 1, depths)
    down = lax.rem(z + depths - 1, depths)
    first = z == 0
    last = z == depths - 1
    pairs, planes = fwd.shape[0], fwd.shape[1]
    count = det.shape[1]

    barrier = pltpu.get_barrier_semaphore()
    for side in (up, down):
        pl.semaphore_signal(barrier, inc=1, device_id={"depth": side}, device_id_type=MESH)
    for step in range(1, groups):
        peer = lax.rem(me + step, groups)
        pl.semaphore_signal(barrier, inc=1, device_id={"src": peer}, device_id_type=MESH)

    row16 = lax.broadcasted_iota(jnp.int32, (16, CHUNK), 0).astype(F32)
    ids = [(row16 + 16.0 * b).astype(BF16) for b in range(N // 16)]
    zero = jnp.zeros((16, CHUNK), BF16)
    one = jnp.ones((16, CHUNK), BF16)

    def spread(row):
        return jnp.broadcast_to(row, (16, CHUNK)).astype(BF16)

    def rows_of(detectors, plane):
        mine = spread(((detectors >> 7) - plane * N).astype(F32))
        return [jnp.where(mine == ids[b], one, zero) for b in range(N // 16)]

    def select(chunk, wanted, fresh):
        start = pl.multiple_of(chunk * CHUNK, CHUNK)
        detectors = det[:, pl.ds(start, CHUNK)]
        if fresh:
            column = spread((detectors & (N - 1)).astype(F32))
            weights = []
            for p in range(pairs):
                value = res[p:p + 1, pl.ds(start, CHUNK)]
                head = value.astype(BF16).astype(F32)
                weights.append((p, spread(head)))
                weights.append((pairs + p, spread(value - head)))
            for b in range(N // 16):
                hit = column == ids[b]
                for slot, weight in weights:
                    rt[slot * N + 16 * b:slot * N + 16 * b + 16, pl.ds(start, CHUNK)] = (
                        jnp.where(hit, weight, zero))
        rows = []
        for plane in wanted:
            rows += rows_of(detectors, plane)
        onehot = jnp.concatenate(rows, axis=0)
        acc[...] += lax.dot_general(
            onehot, rt[:, pl.ds(start, CHUNK)], (((1,), (1,)), ((), ())),
            preferred_element_type=F32)

    def run(begin, end, wanted, fresh):
        def step(chunk, carry):
            select(chunk, wanted, fresh)
            return carry
        lax.fori_loop(begin, end, step, 0)

    def source(slot, p):
        rows = slice(slot * N, (slot + 1) * N)
        return acc[rows, p * N:(p + 1) * N] + acc[rows, (pairs + p) * N:(pairs + p + 1) * N]

    chunks = count // CHUNK
    acc[...] = jnp.zeros_like(acc)
    run(0, chunks // 4, (0, planes - 1), True)

    pl.semaphore_wait(barrier, groups + 1)
    lab_up = pltpu.make_async_remote_copy(
        labels.at[planes - 1], lab_h.at[0], lab_s.at[0], lab_r.at[0],
        device_id={"depth": up}, device_id_type=MESH)
    lab_down = pltpu.make_async_remote_copy(
        labels.at[0], lab_h.at[1], lab_s.at[1], lab_r.at[1],
        device_id={"depth": down}, device_id_type=MESH)
    lab_up.start()
    lab_down.start()

    run(chunks // 4, chunks, (0, planes - 1), True)

    lane = lax.broadcasted_iota(jnp.int32, (N, N), 1)
    row = lax.broadcasted_iota(jnp.int32, (N, N), 0)
    taus = [tau[index[p]] for p in range(pairs)]
    for k in range(planes):
        diff[k] = lookup(dtab, labels[k], dtab.shape[0])
    lab_up.wait()
    lab_down.wait()
    below = jnp.where(first, 0.0, lookup(dtab, lab_h[0], dtab.shape[0]))
    above = jnp.where(last, 0.0, lookup(dtab, lab_h[1], dtab.shape[0]))
    gz[0] = jnp.where(first, 0.0, 0.5 * (below + diff[0]))
    for k in range(1, planes):
        gz[k] = 0.5 * (diff[k - 1] + diff[k])
    gz[planes] = jnp.where(last, 0.0, 0.5 * (diff[planes - 1] + above))
    for k in range(planes):
        here = diff[k]
        right = jnp.where(lane < N - 1, pltpu.roll(here, N - 1, 1), 0.0)
        left = jnp.where(lane > 0, pltpu.roll(here, 1, 1), 0.0)
        south = jnp.where(row < N - 1, pltpu.roll(here, N - 1, 0), 0.0)
        north = jnp.where(row > 0, pltpu.roll(here, 1, 0), 0.0)
        gx[k] = jnp.where(lane < N - 1, 0.5 * (here + right), 0.0)
        gy[k] = jnp.where(row < N - 1, 0.5 * (here + south), 0.0)
        under = below if k == 0 else diff[k - 1]
        over = above if k == planes - 1 else diff[k + 1]
        faces = 3.0 * here + 0.5 * ((left + right) + (north + south) + (under + over))
        base = lookup(atab, labels[k], atab.shape[0]) + faces
        for p in range(pairs):
            inv[k, p] = 1.0 / (base + taus[p] * flow[k])

    ends = (0, planes - 1)
    inner = tuple(range(1, planes - 1))

    def begin(slot, k):
        for p in range(pairs):
            d0[k, p] = source(slot, p) * inv[k, p] * (1.0 / CENTRE)

    def exchange(field, halo, send, receive):
        lift = pltpu.make_async_remote_copy(
            field.at[planes - 1], halo.at[0], send.at[0], receive.at[0],
            device_id={"depth": up}, device_id_type=MESH)
        drop = pltpu.make_async_remote_copy(
            field.at[0], halo.at[1], send.at[1], receive.at[1],
            device_id={"depth": down}, device_id_type=MESH)
        lift.start()
        drop.start()
        return lift, drop

    def gather(field, halo, k, p):
        here = field[k, p]
        under = halo[0, p] if k == 0 else field[k - 1, p]
        over = halo[1, p] if k == planes - 1 else field[k + 1, p]
        total = gz[k] * under + gz[k + 1] * over
        fx, fy = gx[k], gy[k]
        total += fx * pltpu.roll(here, N - 1, 1) + pltpu.roll(fx * here, 1, 1)
        total += fy * pltpu.roll(here, N - 1, 0) + pltpu.roll(fy * here, 1, 0)
        return total

    def advance(k):
        for p in range(pairs):
            old = d0[k, p]
            ratio = (CENTRE - 1.0) * old + inv[k, p] * gather(d0, d0h, k, p)
            q1[k, p] = ratio
            d1[k, p] = (RHO1 * RHO0) * old + (2.0 * RHO1 / HALF) * ratio

    def finish(k):
        total = None
        for p in range(pairs):
            old = d1[k, p]
            ratio = q1[k, p] - old + inv[k, p] * gather(d1, d1h, k, p)
            field = d0[k, p] + (1.0 + RHO2 * RHO1) * old + (2.0 * RHO2 / HALF) * ratio
            coef = -(wgt[index[p]] * taus[p])
            term = coef * fwd[p, k].astype(F32) * field
            total = term if total is None else total + term
        return total

    rows_out = N // groups

    def scatter(phase, low, high):
        sent = []
        for step in range(1, groups):
            peer = lax.rem(me + step, groups)
            rows = pl.ds(pl.multiple_of(peer * rows_out, rows_out), rows_out)
            copy = pltpu.make_async_remote_copy(
                part.at[low:high, rows, :], recv.at[step - 1, low:high],
                rs_s.at[phase, step - 1], rs_r.at[phase, step - 1],
                device_id={"src": peer}, device_id_type=MESH)
            copy.start()
            sent.append(copy)
        return sent

    for slot, k in enumerate(ends):
        begin(slot, k)
    sent0 = exchange(d0, d0h, d0_s, d0_r)

    acc[...] = jnp.zeros_like(acc)
    run(0, chunks, inner, False)
    for slot, k in enumerate(inner):
        begin(slot, k)
    for copy in sent0:
        copy.wait()
    for k in ends:
        advance(k)
    sent1 = exchange(d1, d1h, d1_s, d1_r)
    for k in inner:
        advance(k)
    order = inner + ends
    for slot, k in enumerate(inner):
        part[slot] = finish(k)
    sums = scatter(0, 0, len(inner))
    for copy in sent1:
        copy.wait()
    for slot, k in enumerate(ends):
        part[len(inner) + slot] = finish(k)
    sums += scatter(1, len(inner), planes)
    for copy in sums:
        copy.wait()
    own = pl.ds(pl.multiple_of(me * rows_out, rows_out), rows_out)
    for slot, k in enumerate(order):
        total = part[slot, own, :]
        for step in range(groups - 1):
            total = total + recv[step, slot]
        out[k] = total


def body(
    forward, detectors, residuals, delay_index, labels, blood_flow,
    diff_table, absorb_table, delay_tau, delay_weight,
):
    groups = lax.axis_size("src")
    depths = lax.axis_size("depth")
    pairs, planes = forward.shape[0], forward.shape[1]
    count = detectors.shape[0]
    vmem = pl.BlockSpec(memory_space=pltpu.VMEM)
    smem = pl.BlockSpec(memory_space=pltpu.SMEM)
    dma = pltpu.SemaphoreType.DMA
    plane = lambda *lead: pltpu.VMEM(lead + (N, N), F32)
    return pl.pallas_call(
        functools.partial(kernel, groups, depths),
        out_shape=jax.ShapeDtypeStruct((planes, N // groups, N), F32),
        in_specs=[vmem] * 5 + [smem] * 5,
        out_specs=vmem,
        scratch_shapes=[
            pltpu.VMEM((2 * pairs * N, count), BF16),
            pltpu.VMEM((2 * N, 2 * pairs * N), F32),
            pltpu.VMEM((2, N, N), jnp.int32),
            plane(planes),
            plane(planes, pairs),
            plane(planes),
            plane(planes),
            plane(planes + 1),
            plane(planes, pairs),
            plane(planes, pairs),
            plane(planes, pairs),
            plane(2, pairs),
            plane(2, pairs),
            plane(planes),
            pltpu.VMEM((groups - 1, planes, N // groups, N), F32),
            dma((2,)), dma((2,)), dma((2,)), dma((2,)), dma((2,)), dma((2,)),
            dma((2, groups - 1)), dma((2, groups - 1)),
        ],
        compiler_params=pltpu.CompilerParams(collective_id=0, has_side_effects=True),
        name="flow_gradient",
    )(
        forward, detectors.reshape(1, count), residuals, labels, blood_flow,
        delay_index, diff_table, absorb_table, delay_tau, delay_weight,
    )


def solution(mesh):
    placed = (
        P("src", "depth", None, None),
        P("depth"),
        P("src", "depth"),
        P("src"),
        P("depth", None, None),
        P("depth", None, None),
        P(),
        P(),
        P(),
        P(),
    )
    return jax.shard_map(
        body, mesh=mesh, in_specs=placed, out_specs=P("depth", "src", None), check_vma=False
    )
```

```python
import functools

import jax
import jax.numpy as jnp
from jax import lax
from jax.experimental import pallas as pl
from jax.experimental.pallas import tpu as pltpu
from jax.sharding import PartitionSpec as P

SPECTRUM_LOW = 0.1
SPECTRUM_HIGH = 2.0
CENTRE = 0.5 * (SPECTRUM_HIGH + SPECTRUM_LOW)
HALF = 0.5 * (SPECTRUM_HIGH - SPECTRUM_LOW)
SIGMA = CENTRE / HALF
RHO0 = 1.0 / SIGMA
RHO1 = 1.0 / (2.0 * SIGMA - RHO0)
RHO2 = 1.0 / (2.0 * SIGMA - RHO1)

N = 128
CHUNK = 4096
MESH = pl.DeviceIdType.MESH
F32 = jnp.float32
BF16 = jnp.bfloat16


def lookup(table, labels, count):
    value = jnp.zeros(labels.shape, F32)
    for entry in range(count):
        value = jnp.where(labels == entry, table[entry], value)
    return value


def kernel(
    groups, depths,
    fwd_in, det, res, labels_in, flow_in, index, dtab, atab, tau, wgt,
    out,
    fwd, labels, flow, rt, acc, lab_h, flow_h, diff, inv, gx, gy, gz,
    src, src_h, d0, d0_far, d1, q1, part, recv,
    in_s, lab_s, lab_r, flow_s, flow_r, src_s, src_r, far_s, far_r, rs_s, rs_r,
):
    me = lax.axis_index("src")
    z = lax.axis_index("depth")
    up = lax.rem(z + 1, depths)
    down = lax.rem(z + depths - 1, depths)
    first = z == 0
    last = z == depths - 1
    pairs, planes = fwd.shape[0], fwd.shape[1]
    count = det.shape[1]

    barrier = pltpu.get_barrier_semaphore()
    for side in (up, down):
        pl.semaphore_signal(barrier, inc=1, device_id={"depth": side}, device_id_type=MESH)
    for step in range(1, groups):
        peer = lax.rem(me + step, groups)
        pl.semaphore_signal(barrier, inc=1, device_id={"src": peer}, device_id_type=MESH)
    loads = [
        pltpu.make_async_copy(labels_in, labels, in_s.at[0]),
        pltpu.make_async_copy(flow_in, flow, in_s.at[1]),
        pltpu.make_async_copy(fwd_in, fwd, in_s.at[2]),
    ]
    for copy in loads:
        copy.start()

    def shift(to_up, from_below, to_down, from_above, send, receive):
        pair = (
            pltpu.make_async_remote_copy(
                to_up, from_below, send.at[0], receive.at[0],
                device_id={"depth": up}, device_id_type=MESH),
            pltpu.make_async_remote_copy(
                to_down, from_above, send.at[1], receive.at[1],
                device_id={"depth": down}, device_id_type=MESH),
        )
        for copy in pair:
            copy.start()
        return pair

    def settle(copies):
        for copy in copies:
            copy.wait()

    row16 = lax.broadcasted_iota(jnp.int32, (16, CHUNK), 0).astype(F32)
    ids = [(row16 + 16.0 * b).astype(BF16) for b in range(N // 16)]
    zero = jnp.zeros((16, CHUNK), BF16)
    one = jnp.ones((16, CHUNK), BF16)

    def spread(row):
        return jnp.broadcast_to(row, (16, CHUNK)).astype(BF16)

    def rows_of(detectors, plane):
        mine = spread(((detectors >> 7) - plane * N).astype(F32))
        return [jnp.where(mine == ids[b], one, zero) for b in range(N // 16)]

    def select(chunk, wanted, fresh):
        start = pl.multiple_of(chunk * CHUNK, CHUNK)
        detectors = det[:, pl.ds(start, CHUNK)]
        if fresh:
            column = spread((detectors & (N - 1)).astype(F32))
            weights = []
            for p in range(pairs):
                value = res[p:p + 1, pl.ds(start, CHUNK)]
                head = value.astype(BF16).astype(F32)
                weights.append((p, spread(head)))
                weights.append((pairs + p, spread(value - head)))
            for b in range(N // 16):
                hit = column == ids[b]
                for slot, weight in weights:
                    rt[slot * N + 16 * b:slot * N + 16 * b + 16, pl.ds(start, CHUNK)] = (
                        jnp.where(hit, weight, zero))
        rows = []
        for plane in wanted:
            rows += rows_of(detectors, plane)
        onehot = jnp.concatenate(rows, axis=0)
        acc[...] += lax.dot_general(
            onehot, rt[:, pl.ds(start, CHUNK)], (((1,), (1,)), ((), ())),
            preferred_element_type=F32)

    def run(begin, end, wanted, fresh):
        def step(chunk, carry):
            select(chunk, wanted, fresh)
            return carry
        lax.fori_loop(begin, end, step, 0)

    def source(slot, p):
        rows = slice(slot * N, (slot + 1) * N)
        return acc[rows, p * N:(p + 1) * N] + acc[rows, (pairs + p) * N:(pairs + p + 1) * N]

    chunks = count // CHUNK
    ends = (0, planes - 1)
    inner = tuple(range(1, planes - 1))
    below, above = planes, planes + 1

    acc[...] = jnp.zeros_like(acc)
    run(0, 1, ends, True)
    pl.semaphore_wait(barrier, groups + 1)
    for copy in loads[:2]:
        copy.wait()
    sent_labels = shift(
        labels.at[planes - 2:planes], lab_h.at[0], labels.at[0:2], lab_h.at[1], lab_s, lab_r)
    sent_flow = shift(
        flow.at[planes - 1], flow_h.at[0], flow.at[0], flow_h.at[1], flow_s, flow_r)
    run(1, chunks, ends, True)
    for slot in range(2):
        for p in range(pairs):
            src[slot, p] = source(slot, p)
    sent_src = shift(src.at[1], src_h.at[0], src.at[0], src_h.at[1], src_s, src_r)

    lane = lax.broadcasted_iota(jnp.int32, (N, N), 1)
    row = lax.broadcasted_iota(jnp.int32, (N, N), 0)
    taus = [tau[index[p]] for p in range(pairs)]

    def coefficients(k, here, under, over, label, stream):
        right = jnp.where(lane < N - 1, pltpu.roll(here, N - 1, 1), 0.0)
        left = jnp.where(lane > 0, pltpu.roll(here, 1, 1), 0.0)
        south = jnp.where(row < N - 1, pltpu.roll(here, N - 1, 0), 0.0)
        north = jnp.where(row > 0, pltpu.roll(here, 1, 0), 0.0)
        gx[k] = jnp.where(lane < N - 1, 0.5 * (here + right), 0.0)
        gy[k] = jnp.where(row < N - 1, 0.5 * (here + south), 0.0)
        faces = 3.0 * here + 0.5 * ((left + right) + (north + south) + (under + over))
        base = lookup(atab, label, atab.shape[0]) + faces
        for p in range(pairs):
            inv[k, p] = 1.0 / (base + taus[p] * stream)

    def gather(field, k, p, lower, upper, under, over):
        here = field[k, p]
        fx, fy = gx[k], gy[k]
        total = lower * under + upper * over
        total += fx * pltpu.roll(here, N - 1, 1) + pltpu.roll(fx * here, 1, 1)
        total += fy * pltpu.roll(here, N - 1, 0) + pltpu.roll(fy * here, 1, 0)
        return total

    def inside(field, k, p):
        under = field[below if k == 0 else k - 1, p]
        over = field[above if k == planes - 1 else k + 1, p]
        return gather(field, k, p, gz[k], gz[k + 1], under, over)

    def advance(k, p, shared):
        old = d0[k, p]
        ratio = (CENTRE - 1.0) * old + inv[k, p] * shared
        d1[k, p] = (RHO1 * RHO0) * old + (2.0 * RHO1 / HALF) * ratio
        if k < planes:
            q1[k, p] = ratio

    def finish(k):
        total = None
        for p in range(pairs):
            old = d1[k, p]
            ratio = q1[k, p] - old + inv[k, p] * inside(d1, k, p)
            field = d0[k, p] + (1.0 + RHO2 * RHO1) * old + (2.0 * RHO2 / HALF) * ratio
            coef = -(wgt[index[p]] * taus[p])
            term = coef * fwd[p, k].astype(F32) * field
            total = term if total is None else total + term
        return total

    rows_out = N // groups

    def scatter(phase, low, high):
        sent = []
        for step in range(1, groups):
            peer = lax.rem(me + step, groups)
            rows = pl.ds(pl.multiple_of(peer * rows_out, rows_out), rows_out)
            copy = pltpu.make_async_remote_copy(
                part.at[low:high, rows, :], recv.at[step - 1, low:high],
                rs_s.at[phase, step - 1], rs_r.at[phase, step - 1],
                device_id={"src": peer}, device_id_type=MESH)
            copy.start()
            sent.append(copy)
        return sent

    for k in range(planes):
        diff[k] = lookup(dtab, labels[k], dtab.shape[0])
    for k in range(1, planes):
        gz[k] = 0.5 * (diff[k - 1] + diff[k])
    for k in inner:
        coefficients(k, diff[k], diff[k - 1], diff[k + 1], labels[k], flow[k])

    acc[...] = jnp.zeros_like(acc)
    run(0, chunks, inner, False)
    for slot, k in enumerate(inner):
        for p in range(pairs):
            d0[k, p] = source(slot, p) * inv[k, p] * (1.0 / CENTRE)
    sent_far = shift(
        d0.at[planes - 2], d0_far.at[0], d0.at[1], d0_far.at[1], far_s, far_r)

    settle(sent_labels)
    settle(sent_flow)
    halo = [[lookup(dtab, lab_h[s, i], dtab.shape[0]) for i in range(2)] for s in range(2)]
    low = jnp.where(first, 0.0, halo[0][1])
    high = jnp.where(last, 0.0, halo[1][0])
    gz[0] = jnp.where(first, 0.0, 0.5 * (low + diff[0]))
    gz[planes] = jnp.where(last, 0.0, 0.5 * (diff[planes - 1] + high))
    coefficients(0, diff[0], low, diff[1], labels[0], flow[0])
    coefficients(planes - 1, diff[planes - 1], diff[planes - 2], high,
                 labels[planes - 1], flow[planes - 1])
    coefficients(below, halo[0][1], halo[0][0], diff[0], lab_h[0, 1], flow_h[0])
    coefficients(above, halo[1][0], diff[planes - 1], halo[1][1], lab_h[1, 0], flow_h[1])
    far = (0.5 * (halo[0][0] + halo[0][1]), 0.5 * (halo[1][0] + halo[1][1]))
    gz[planes + 1] = far[0]
    gz[planes + 2] = far[1]
    for slot, k in enumerate(ends):
        for p in range(pairs):
            d0[k, p] = src[slot, p] * inv[k, p] * (1.0 / CENTRE)
    for k in inner:
        for p in range(pairs):
            advance(k, p, inside(d0, k, p))
    settle(sent_src)
    for side, k in enumerate((below, above)):
        for p in range(pairs):
            d0[k, p] = src_h[side, p] * inv[k, p] * (1.0 / CENTRE)
    for k in ends:
        for p in range(pairs):
            advance(k, p, inside(d0, k, p))
    copy = loads[2]
    copy.wait()
    order = inner + ends
    for slot, k in enumerate(inner):
        part[slot] = finish(k)
    sums = scatter(0, 0, len(inner))
    settle(sent_far)
    for p in range(pairs):
        advance(below, p, gather(
            d0, below, p, gz[planes + 1], gz[0], d0_far[0, p], d0[0, p]))
        advance(above, p, gather(
            d0, above, p, gz[planes], gz[planes + 2], d0[planes - 1, p], d0_far[1, p]))
    for slot, k in enumerate(ends):
        part[len(inner) + slot] = finish(k)
    sums += scatter(1, len(inner), planes)
    settle(sums)
    own = pl.ds(pl.multiple_of(me * rows_out, rows_out), rows_out)
    for slot, k in enumerate(order):
        total = part[slot, own, :]
        for step in range(groups - 1):
            total = total + recv[step, slot]
        out[k] = total


def body(
    forward, detectors, residuals, delay_index, labels, blood_flow,
    diff_table, absorb_table, delay_tau, delay_weight,
):
    groups = lax.axis_size("src")
    depths = lax.axis_size("depth")
    pairs, planes = forward.shape[0], forward.shape[1]
    count = detectors.shape[0]
    vmem = pl.BlockSpec(memory_space=pltpu.VMEM)
    hbm = pl.BlockSpec(memory_space=pl.ANY)
    smem = pl.BlockSpec(memory_space=pltpu.SMEM)
    dma = pltpu.SemaphoreType.DMA
    plane = lambda *lead: pltpu.VMEM(lead + (N, N), F32)
    return pl.pallas_call(
        functools.partial(kernel, groups, depths),
        out_shape=jax.ShapeDtypeStruct((planes, N // groups, N), F32),
        in_specs=[hbm, vmem, vmem, hbm, hbm] + [smem] * 5,
        out_specs=vmem,
        scratch_shapes=[
            pltpu.VMEM((pairs, planes, N, N), BF16),
            pltpu.VMEM((planes, N, N), jnp.int32),
            plane(planes),
            pltpu.VMEM((2 * pairs * N, count), BF16),
            pltpu.VMEM((2 * N, 2 * pairs * N), F32),
            pltpu.VMEM((2, 2, N, N), jnp.int32),
            plane(2),
            plane(planes),
            plane(planes + 2, pairs),
            plane(planes + 2),
            plane(planes + 2),
            plane(planes + 3),
            plane(2, pairs),
            plane(2, pairs),
            plane(planes + 2, pairs),
            plane(2, pairs),
            plane(planes + 2, pairs),
            plane(planes, pairs),
            plane(planes),
            pltpu.VMEM((groups - 1, planes, N // groups, N), F32),
            dma((3,)), dma((2,)), dma((2,)), dma((2,)), dma((2,)), dma((2,)), dma((2,)),
            dma((2,)), dma((2,)),
            dma((2, groups - 1)), dma((2, groups - 1)),
        ],
        compiler_params=pltpu.CompilerParams(collective_id=0, has_side_effects=True),
        name="flow_gradient",
    )(
        forward, detectors.reshape(1, count), residuals, labels, blood_flow,
        delay_index, diff_table, absorb_table, delay_tau, delay_weight,
    )


def solution(mesh):
    placed = (
        P("src", "depth", None, None),
        P("depth"),
        P("src", "depth"),
        P("src"),
        P("depth", None, None),
        P("depth", None, None),
        P(),
        P(),
        P(),
        P(),
    )
    return jax.shard_map(
        body, mesh=mesh, in_specs=placed, out_specs=P("depth", "src", None), check_vma=False
    )
```

```python
import functools

import jax
import jax.numpy as jnp
from jax import lax
from jax.experimental import pallas as pl
from jax.experimental.pallas import tpu as pltpu
from jax.sharding import PartitionSpec as P

SPECTRUM_LOW = 0.1
SPECTRUM_HIGH = 2.0
CENTRE = 0.5 * (SPECTRUM_HIGH + SPECTRUM_LOW)
HALF = 0.5 * (SPECTRUM_HIGH - SPECTRUM_LOW)
SIGMA = CENTRE / HALF
RHO0 = 1.0 / SIGMA
RHO1 = 1.0 / (2.0 * SIGMA - RHO0)
RHO2 = 1.0 / (2.0 * SIGMA - RHO1)

N = 128
CHUNK = 4096
MESH = pl.DeviceIdType.MESH
F32 = jnp.float32
BF16 = jnp.bfloat16


def lookup(table, labels, count):
    value = jnp.zeros(labels.shape, F32)
    for entry in range(count):
        value = jnp.where(labels == entry, table[entry], value)
    return value


def kernel(
    groups, depths,
    fwd_in, det, res, labels_in, flow_in, index, dtab, atab, tau, wgt,
    out,
    fwd, labels, flow, rt, acc, lab_h, flow_h, diff, inv, gx, gy, gz,
    src, src_h, d0, d0_far, d1, q1, part, recv,
    in_s, lab_s, lab_r, flow_s, flow_r, src_s, src_r, far_s, far_r, rs_s, rs_r,
):
    me = lax.axis_index("src")
    z = lax.axis_index("depth")
    up = jnp.minimum(z + 1, depths - 1)
    down = jnp.maximum(z - 1, 0)
    first = z == 0
    last = z == depths - 1
    pairs, planes = fwd.shape[0], fwd.shape[1]
    count = det.shape[1]

    barrier = pltpu.get_barrier_semaphore()
    inside_low = z > 0
    inside_high = z < depths - 1
    for has, side in ((inside_high, up), (inside_low, down)):
        @pl.when(has)
        def _(side=side):
            pl.semaphore_signal(barrier, inc=1, device_id={"depth": side}, device_id_type=MESH)
    for step in range(1, groups):
        peer = lax.rem(me + step, groups)
        pl.semaphore_signal(barrier, inc=1, device_id={"src": peer}, device_id_type=MESH)
    loads = [
        pltpu.make_async_copy(labels_in, labels, in_s.at[0]),
        pltpu.make_async_copy(flow_in, flow, in_s.at[1]),
        pltpu.make_async_copy(fwd_in, fwd, in_s.at[2]),
    ]
    for copy in loads:
        copy.start()

    def shift(to_up, from_below, to_down, from_above, send, receive):
        pair = (
            pltpu.make_async_remote_copy(
                to_up, from_below, send.at[0], receive.at[0],
                device_id={"depth": up}, device_id_type=MESH),
            pltpu.make_async_remote_copy(
                to_down, from_above, send.at[1], receive.at[1],
                device_id={"depth": down}, device_id_type=MESH),
        )
        pl.when(inside_high)(pair[0].start)
        pl.when(inside_low)(pair[1].start)
        return pair

    def settle_halo(pair):
        @pl.when(inside_high)
        def _():
            pair[0].wait_send()
            pair[1].wait_recv()

        @pl.when(inside_low)
        def _():
            pair[0].wait_recv()
            pair[1].wait_send()

    for has, side in ((first, 0), (last, 1)):
        @pl.when(has)
        def _(side=side):
            lab_h[side] = jnp.zeros(lab_h.shape[1:], jnp.int32)
            flow_h[side] = jnp.ones(flow_h.shape[1:], F32)
            src_h[side] = jnp.zeros(src_h.shape[1:], F32)
            d0_far[side] = jnp.zeros(d0_far.shape[1:], F32)

    row16 = lax.broadcasted_iota(jnp.int32, (16, CHUNK), 0).astype(F32)
    ids = [(row16 + 16.0 * b).astype(BF16) for b in range(N // 16)]
    zero = jnp.zeros((16, CHUNK), BF16)
    one = jnp.ones((16, CHUNK), BF16)

    def spread(row):
        return jnp.broadcast_to(row, (16, CHUNK)).astype(BF16)

    def rows_of(detectors, plane):
        mine = spread(((detectors >> 7) - plane * N).astype(F32))
        return [jnp.where(mine == ids[b], one, zero) for b in range(N // 16)]

    def select(chunk, wanted, fresh):
        start = pl.multiple_of(chunk * CHUNK, CHUNK)
        detectors = det[:, pl.ds(start, CHUNK)]
        if fresh:
            column = spread((detectors & (N - 1)).astype(F32))
            weights = []
            for p in range(pairs):
                value = res[p:p + 1, pl.ds(start, CHUNK)]
                head = value.astype(BF16).astype(F32)
                weights.append((p, spread(head)))
                weights.append((pairs + p, spread(value - head)))
            for b in range(N // 16):
                hit = column == ids[b]
                for slot, weight in weights:
                    rt[slot * N + 16 * b:slot * N + 16 * b + 16, pl.ds(start, CHUNK)] = (
                        jnp.where(hit, weight, zero))
        rows = []
        for plane in wanted:
            rows += rows_of(detectors, plane)
        onehot = jnp.concatenate(rows, axis=0)
        acc[...] += lax.dot_general(
            onehot, rt[:, pl.ds(start, CHUNK)], (((1,), (1,)), ((), ())),
            preferred_element_type=F32)

    def run(begin, end, wanted, fresh):
        def step(chunk, carry):
            select(chunk, wanted, fresh)
            return carry
        lax.fori_loop(begin, end, step, 0)

    def source(slot, p):
        rows = slice(slot * N, (slot + 1) * N)
        return acc[rows, p * N:(p + 1) * N] + acc[rows, (pairs + p) * N:(pairs + p + 1) * N]

    chunks = count // CHUNK
    ends = (0, planes - 1)
    inner = tuple(range(1, planes - 1))
    below, above = planes, planes + 1

    acc[...] = jnp.zeros_like(acc)
    run(0, 1, ends, True)
    pl.semaphore_wait(
        barrier, groups - 1 + jnp.minimum(z, 1) + jnp.minimum(depths - 1 - z, 1))
    for copy in loads[:2]:
        copy.wait()
    sent_labels = shift(
        labels.at[planes - 2:planes], lab_h.at[0], labels.at[0:2], lab_h.at[1], lab_s, lab_r)
    sent_flow = shift(
        flow.at[planes - 1], flow_h.at[0], flow.at[0], flow_h.at[1], flow_s, flow_r)
    run(1, chunks, ends, True)
    for slot in range(2):
        for p in range(pairs):
            src[slot, p] = source(slot, p)
    sent_src = shift(src.at[1], src_h.at[0], src.at[0], src_h.at[1], src_s, src_r)

    lane = lax.broadcasted_iota(jnp.int32, (N, N), 1)
    row = lax.broadcasted_iota(jnp.int32, (N, N), 0)
    taus = [tau[index[p]] for p in range(pairs)]

    def coefficients(k, here, under, over, label, stream):
        right = jnp.where(lane < N - 1, pltpu.roll(here, N - 1, 1), 0.0)
        left = jnp.where(lane > 0, pltpu.roll(here, 1, 1), 0.0)
        south = jnp.where(row < N - 1, pltpu.roll(here, N - 1, 0), 0.0)
        north = jnp.where(row > 0, pltpu.roll(here, 1, 0), 0.0)
        gx[k] = jnp.where(lane < N - 1, 0.5 * (here + right), 0.0)
        gy[k] = jnp.where(row < N - 1, 0.5 * (here + south), 0.0)
        faces = 3.0 * here + 0.5 * ((left + right) + (north + south) + (under + over))
        base = lookup(atab, label, atab.shape[0]) + faces
        for p in range(pairs):
            inv[k, p] = 1.0 / (base + taus[p] * stream)

    def gather(field, k, p, lower, upper, under, over):
        here = field[k, p]
        fx, fy = gx[k], gy[k]
        total = lower * under + upper * over
        total += fx * pltpu.roll(here, N - 1, 1) + pltpu.roll(fx * here, 1, 1)
        total += fy * pltpu.roll(here, N - 1, 0) + pltpu.roll(fy * here, 1, 0)
        return total

    def inside(field, k, p):
        under = field[below if k == 0 else k - 1, p]
        over = field[above if k == planes - 1 else k + 1, p]
        return gather(field, k, p, gz[k], gz[k + 1], under, over)

    def advance(k, p, shared):
        old = d0[k, p]
        ratio = (CENTRE - 1.0) * old + inv[k, p] * shared
        d1[k, p] = (RHO1 * RHO0) * old + (2.0 * RHO1 / HALF) * ratio
        if k < planes:
            q1[k, p] = ratio

    def finish(k):
        total = None
        for p in range(pairs):
            old = d1[k, p]
            ratio = q1[k, p] - old + inv[k, p] * inside(d1, k, p)
            field = d0[k, p] + (1.0 + RHO2 * RHO1) * old + (2.0 * RHO2 / HALF) * ratio
            coef = -(wgt[index[p]] * taus[p])
            term = coef * fwd[p, k].astype(F32) * field
            total = term if total is None else total + term
        return total

    rows_out = N // groups

    def scatter(phase, low, high):
        sent = []
        for step in range(1, groups):
            peer = lax.rem(me + step, groups)
            rows = pl.ds(pl.multiple_of(peer * rows_out, rows_out), rows_out)
            copy = pltpu.make_async_remote_copy(
                part.at[low:high, rows, :], recv.at[step - 1, low:high],
                rs_s.at[phase, step - 1], rs_r.at[phase, step - 1],
                device_id={"src": peer}, device_id_type=MESH)
            copy.start()
            sent.append(copy)
        return sent

    for k in range(planes):
        diff[k] = lookup(dtab, labels[k], dtab.shape[0])
    for k in range(1, planes):
        gz[k] = 0.5 * (diff[k - 1] + diff[k])
    for k in inner:
        coefficients(k, diff[k], diff[k - 1], diff[k + 1], labels[k], flow[k])

    acc[...] = jnp.zeros_like(acc)
    run(0, chunks, inner, False)
    for slot, k in enumerate(inner):
        for p in range(pairs):
            d0[k, p] = source(slot, p) * inv[k, p] * (1.0 / CENTRE)
    sent_far = shift(
        d0.at[planes - 2], d0_far.at[0], d0.at[1], d0_far.at[1], far_s, far_r)

    settle_halo(sent_labels)
    settle_halo(sent_flow)
    halo = [[lookup(dtab, lab_h[s, i], dtab.shape[0]) for i in range(2)] for s in range(2)]
    low = jnp.where(first, 0.0, halo[0][1])
    high = jnp.where(last, 0.0, halo[1][0])
    gz[0] = jnp.where(first, 0.0, 0.5 * (low + diff[0]))
    gz[planes] = jnp.where(last, 0.0, 0.5 * (diff[planes - 1] + high))
    coefficients(0, diff[0], low, diff[1], labels[0], flow[0])
    coefficients(planes - 1, diff[planes - 1], diff[planes - 2], high,
                 labels[planes - 1], flow[planes - 1])
    coefficients(below, halo[0][1], halo[0][0], diff[0], lab_h[0, 1], flow_h[0])
    coefficients(above, halo[1][0], diff[planes - 1], halo[1][1], lab_h[1, 0], flow_h[1])
    far = (0.5 * (halo[0][0] + halo[0][1]), 0.5 * (halo[1][0] + halo[1][1]))
    gz[planes + 1] = far[0]
    gz[planes + 2] = far[1]
    for slot, k in enumerate(ends):
        for p in range(pairs):
            d0[k, p] = src[slot, p] * inv[k, p] * (1.0 / CENTRE)
    for k in inner:
        for p in range(pairs):
            advance(k, p, inside(d0, k, p))
    settle_halo(sent_src)
    for side, k in enumerate((below, above)):
        for p in range(pairs):
            d0[k, p] = src_h[side, p] * inv[k, p] * (1.0 / CENTRE)
    for k in ends:
        for p in range(pairs):
            advance(k, p, inside(d0, k, p))
    copy = loads[2]
    copy.wait()
    order = inner + ends
    for slot, k in enumerate(inner):
        part[slot] = finish(k)
    sums = scatter(0, 0, len(inner))
    settle_halo(sent_far)
    for p in range(pairs):
        advance(below, p, gather(
            d0, below, p, gz[planes + 1], gz[0], d0_far[0, p], d0[0, p]))
        advance(above, p, gather(
            d0, above, p, gz[planes], gz[planes + 2], d0[planes - 1, p], d0_far[1, p]))
    for slot, k in enumerate(ends):
        part[len(inner) + slot] = finish(k)
    sums += scatter(1, len(inner), planes)
    for copy in sums:
        copy.wait()
    own = pl.ds(pl.multiple_of(me * rows_out, rows_out), rows_out)
    for slot, k in enumerate(order):
        total = part[slot, own, :]
        for step in range(groups - 1):
            total = total + recv[step, slot]
        out[k] = total


def body(
    forward, detectors, residuals, delay_index, labels, blood_flow,
    diff_table, absorb_table, delay_tau, delay_weight,
):
    groups = lax.axis_size("src")
    depths = lax.axis_size("depth")
    pairs, planes = forward.shape[0], forward.shape[1]
    count = detectors.shape[0]
    vmem = pl.BlockSpec(memory_space=pltpu.VMEM)
    hbm = pl.BlockSpec(memory_space=pl.ANY)
    smem = pl.BlockSpec(memory_space=pltpu.SMEM)
    dma = pltpu.SemaphoreType.DMA
    plane = lambda *lead: pltpu.VMEM(lead + (N, N), F32)
    return pl.pallas_call(
        functools.partial(kernel, groups, depths),
        out_shape=jax.ShapeDtypeStruct((planes, N // groups, N), F32),
        in_specs=[hbm, vmem, vmem, hbm, hbm] + [smem] * 5,
        out_specs=vmem,
        scratch_shapes=[
            pltpu.VMEM((pairs, planes, N, N), BF16),
            pltpu.VMEM((planes, N, N), jnp.int32),
            plane(planes),
            pltpu.VMEM((2 * pairs * N, count), BF16),
            pltpu.VMEM((2 * N, 2 * pairs * N), F32),
            pltpu.VMEM((2, 2, N, N), jnp.int32),
            plane(2),
            plane(planes),
            plane(planes + 2, pairs),
            plane(planes + 2),
            plane(planes + 2),
            plane(planes + 3),
            plane(2, pairs),
            plane(2, pairs),
            plane(planes + 2, pairs),
            plane(2, pairs),
            plane(planes + 2, pairs),
            plane(planes, pairs),
            plane(planes),
            pltpu.VMEM((groups - 1, planes, N // groups, N), F32),
            dma((3,)), dma((2,)), dma((2,)), dma((2,)), dma((2,)), dma((2,)), dma((2,)),
            dma((2,)), dma((2,)),
            dma((2, groups - 1)), dma((2, groups - 1)),
        ],
        compiler_params=pltpu.CompilerParams(collective_id=0, has_side_effects=True),
        name="flow_gradient",
    )(
        forward, detectors.reshape(1, count), residuals, labels, blood_flow,
        delay_index, diff_table, absorb_table, delay_tau, delay_weight,
    )


def solution(mesh):
    placed = (
        P("src", "depth", None, None),
        P("depth"),
        P("src", "depth"),
        P("src"),
        P("depth", None, None),
        P("depth", None, None),
        P(),
        P(),
        P(),
        P(),
    )
    return jax.shard_map(
        body, mesh=mesh, in_specs=placed, out_specs=P("depth", "src", None), check_vma=False
    )
```

```python
import functools

import jax
import jax.numpy as jnp
from jax import lax
from jax.experimental import pallas as pl
from jax.experimental.pallas import tpu as pltpu
from jax.sharding import PartitionSpec as P

SPECTRUM_LOW = 0.1
SPECTRUM_HIGH = 2.0
CENTRE = 0.5 * (SPECTRUM_HIGH + SPECTRUM_LOW)
HALF = 0.5 * (SPECTRUM_HIGH - SPECTRUM_LOW)
SIGMA = CENTRE / HALF
RHO0 = 1.0 / SIGMA
RHO1 = 1.0 / (2.0 * SIGMA - RHO0)
RHO2 = 1.0 / (2.0 * SIGMA - RHO1)

N = 128
CHUNK = 8192
MESH = pl.DeviceIdType.MESH
F32 = jnp.float32
BF16 = jnp.bfloat16


def lookup(table, labels, count):
    value = jnp.zeros(labels.shape, F32)
    for entry in range(count):
        value = jnp.where(labels == entry, table[entry], value)
    return value


def kernel(
    groups, depths,
    fwd_in, det, res, labels_in, flow_in, index, dtab, atab, tau, wgt,
    out,
    fwd, labels, flow, rt, acc, lab_h, flow_h, diff, inv, gx, gy, gz,
    src, src_h, d0, d0_far, d1, q1, part, recv,
    in_s, lab_s, lab_r, flow_s, flow_r, src_s, src_r, far_s, far_r, pass_s, pass_r,
    rs_s, rs_r,
):
    me = lax.axis_index("src")
    z = lax.axis_index("depth")
    up = jnp.minimum(z + 1, depths - 1)
    down = jnp.maximum(z - 1, 0)
    first = z == 0
    last = z == depths - 1
    pairs, planes = fwd.shape[0], fwd.shape[1]
    count = det.shape[1]

    barrier = pltpu.get_barrier_semaphore()
    inside_low = z > 0
    inside_high = z < depths - 1
    for has, side in ((inside_high, up), (inside_low, down)):
        @pl.when(has)
        def _(side=side):
            pl.semaphore_signal(barrier, inc=1, device_id={"depth": side}, device_id_type=MESH)
    for step in range(1, groups):
        peer = lax.rem(me + step, groups)
        pl.semaphore_signal(barrier, inc=1, device_id={"src": peer}, device_id_type=MESH)
    loads = [
        pltpu.make_async_copy(labels_in, labels, in_s.at[0]),
        pltpu.make_async_copy(flow_in, flow, in_s.at[1]),
        pltpu.make_async_copy(fwd_in, fwd, in_s.at[2]),
    ]
    for copy in loads:
        copy.start()

    def shift(to_up, from_below, to_down, from_above, send, receive):
        pair = (
            pltpu.make_async_remote_copy(
                to_up, from_below, send.at[0], receive.at[0],
                device_id={"depth": up}, device_id_type=MESH),
            pltpu.make_async_remote_copy(
                to_down, from_above, send.at[1], receive.at[1],
                device_id={"depth": down}, device_id_type=MESH),
        )
        pl.when(inside_high)(pair[0].start)
        pl.when(inside_low)(pair[1].start)
        return pair

    def settle_halo(pair):
        @pl.when(inside_high)
        def _():
            pair[0].wait_send()
            pair[1].wait_recv()

        @pl.when(inside_low)
        def _():
            pair[0].wait_recv()
            pair[1].wait_send()

    for has, side in ((first, 0), (last, 1)):
        @pl.when(has)
        def _(side=side):
            lab_h[side] = jnp.zeros(lab_h.shape[1:], jnp.int32)
            flow_h[side] = jnp.ones(flow_h.shape[1:], F32)
            src_h[side] = jnp.zeros(src_h.shape[1:], F32)
            d0_far[side] = jnp.zeros(d0_far.shape[1:], F32)

    row16 = lax.broadcasted_iota(jnp.int32, (16, CHUNK), 0).astype(F32)
    ids = [(row16 + 16.0 * b).astype(BF16) for b in range(N // 16)]
    zero = jnp.zeros((16, CHUNK), BF16)
    one = jnp.ones((16, CHUNK), BF16)

    def spread(row):
        return jnp.broadcast_to(row, (16, CHUNK)).astype(BF16)

    def rows_of(detectors, plane):
        mine = spread(((detectors >> 7) - plane * N).astype(F32))
        return [jnp.where(mine == ids[b], one, zero) for b in range(N // 16)]

    def select(chunk, wanted, fresh):
        start = pl.multiple_of(chunk * CHUNK, CHUNK)
        detectors = det[:, pl.ds(start, CHUNK)]
        if fresh:
            column = spread((detectors & (N - 1)).astype(F32))
            weights = []
            for p in range(pairs):
                value = res[p:p + 1, pl.ds(start, CHUNK)]
                head = value.astype(BF16).astype(F32)
                weights.append((p, spread(head)))
                weights.append((pairs + p, spread(value - head)))
            for b in range(N // 16):
                hit = column == ids[b]
                for slot, weight in weights:
                    rt[slot * N + 16 * b:slot * N + 16 * b + 16, pl.ds(start, CHUNK)] = (
                        jnp.where(hit, weight, zero))
        rows = []
        for plane in wanted:
            rows += rows_of(detectors, plane)
        onehot = jnp.concatenate(rows, axis=0)
        acc[...] += lax.dot_general(
            onehot, rt[:, pl.ds(start, CHUNK)], (((1,), (1,)), ((), ())),
            preferred_element_type=F32)

    def run(begin, end, wanted, fresh):
        def step(chunk, carry):
            select(chunk, wanted, fresh)
            return carry
        lax.fori_loop(begin, end, step, 0)

    def source(slot, p):
        rows = slice(slot * N, (slot + 1) * N)
        return acc[rows, p * N:(p + 1) * N] + acc[rows, (pairs + p) * N:(pairs + p + 1) * N]

    chunks = count // CHUNK
    ends = (0, planes - 1)
    inner = tuple(range(1, planes - 1))
    below, above = planes, planes + 1

    acc[...] = jnp.zeros_like(acc)
    run(0, 1, ends, True)
    pl.semaphore_wait(
        barrier, groups - 1 + jnp.minimum(z, 1) + jnp.minimum(depths - 1 - z, 1))
    for copy in loads[:2]:
        copy.wait()
    half = N // 2
    mine = pl.ds(pl.multiple_of(lax.rem(me, 2) * half, half), half)
    twin = me + 1 - 2 * lax.rem(me, 2)
    sent_labels = shift(
        labels.at[planes - 2:planes, mine], lab_h.at[0, :, mine],
        labels.at[0:2, mine], lab_h.at[1, :, mine], lab_s, lab_r)
    sent_flow = shift(
        flow.at[planes - 1, mine], flow_h.at[0, mine],
        flow.at[0, mine], flow_h.at[1, mine], flow_s, flow_r)
    run(1, chunks, ends, True)
    for slot in range(2):
        for p in range(pairs):
            src[slot, p] = source(slot, p)
    sent_src = shift(src.at[1], src_h.at[0], src.at[0], src_h.at[1], src_s, src_r)

    lane = lax.broadcasted_iota(jnp.int32, (N, N), 1)
    row = lax.broadcasted_iota(jnp.int32, (N, N), 0)
    taus = [tau[index[p]] for p in range(pairs)]

    def coefficients(k, here, under, over, label, stream):
        right = jnp.where(lane < N - 1, pltpu.roll(here, N - 1, 1), 0.0)
        left = jnp.where(lane > 0, pltpu.roll(here, 1, 1), 0.0)
        south = jnp.where(row < N - 1, pltpu.roll(here, N - 1, 0), 0.0)
        north = jnp.where(row > 0, pltpu.roll(here, 1, 0), 0.0)
        gx[k] = jnp.where(lane < N - 1, 0.5 * (here + right), 0.0)
        gy[k] = jnp.where(row < N - 1, 0.5 * (here + south), 0.0)
        faces = 3.0 * here + 0.5 * ((left + right) + (north + south) + (under + over))
        base = lookup(atab, label, atab.shape[0]) + faces
        for p in range(pairs):
            inv[k, p] = 1.0 / (base + taus[p] * stream)

    def gather(field, k, p, lower, upper, under, over):
        here = field[k, p]
        fx, fy = gx[k], gy[k]
        total = lower * under + upper * over
        total += fx * pltpu.roll(here, N - 1, 1) + pltpu.roll(fx * here, 1, 1)
        total += fy * pltpu.roll(here, N - 1, 0) + pltpu.roll(fy * here, 1, 0)
        return total

    def inside(field, k, p):
        under = field[below if k == 0 else k - 1, p]
        over = field[above if k == planes - 1 else k + 1, p]
        return gather(field, k, p, gz[k], gz[k + 1], under, over)

    def advance(k, p, shared):
        old = d0[k, p]
        ratio = (CENTRE - 1.0) * old + inv[k, p] * shared
        d1[k, p] = (RHO1 * RHO0) * old + (2.0 * RHO1 / HALF) * ratio
        if k < planes:
            q1[k, p] = ratio

    def finish(k):
        total = None
        for p in range(pairs):
            old = d1[k, p]
            ratio = q1[k, p] - old + inv[k, p] * inside(d1, k, p)
            field = d0[k, p] + (1.0 + RHO2 * RHO1) * old + (2.0 * RHO2 / HALF) * ratio
            coef = -(wgt[index[p]] * taus[p])
            term = coef * fwd[p, k].astype(F32) * field
            total = term if total is None else total + term
        return total

    rows_out = N // groups

    def scatter(phase, low, high):
        sent = []
        for step in range(1, groups):
            peer = lax.rem(me + step, groups)
            rows = pl.ds(pl.multiple_of(peer * rows_out, rows_out), rows_out)
            copy = pltpu.make_async_remote_copy(
                part.at[low:high, rows, :], recv.at[step - 1, low:high],
                rs_s.at[phase, step - 1], rs_r.at[phase, step - 1],
                device_id={"src": peer}, device_id_type=MESH)
            copy.start()
            sent.append(copy)
        return sent

    for k in range(planes):
        diff[k] = lookup(dtab, labels[k], dtab.shape[0])
    for k in range(1, planes):
        gz[k] = 0.5 * (diff[k - 1] + diff[k])
    for k in inner:
        coefficients(k, diff[k], diff[k - 1], diff[k + 1], labels[k], flow[k])

    acc[...] = jnp.zeros_like(acc)
    run(0, chunks // 2, inner, False)
    settle_halo(sent_labels)
    settle_halo(sent_flow)
    relays = [
        pltpu.make_async_remote_copy(
            ref, ref, pass_s.at[slot], pass_r.at[slot],
            device_id={"src": twin}, device_id_type=MESH)
        for slot, ref in enumerate((
            lab_h.at[0, :, mine], flow_h.at[0, mine], lab_h.at[1, :, mine], flow_h.at[1, mine]))
    ]

    def each_relay(act):
        for has, pair in ((inside_low, relays[:2]), (inside_high, relays[2:])):
            @pl.when(has)
            def _(pair=pair):
                for copy in pair:
                    act(copy)

    each_relay(lambda copy: copy.start())
    run(chunks // 2, chunks, inner, False)
    for slot, k in enumerate(inner):
        for p in range(pairs):
            d0[k, p] = source(slot, p) * inv[k, p] * (1.0 / CENTRE)
    sent_far = shift(
        d0.at[planes - 2], d0_far.at[0], d0.at[1], d0_far.at[1], far_s, far_r)

    each_relay(lambda copy: copy.wait())
    halo = [[lookup(dtab, lab_h[s, i], dtab.shape[0]) for i in range(2)] for s in range(2)]
    low = jnp.where(first, 0.0, halo[0][1])
    high = jnp.where(last, 0.0, halo[1][0])
    gz[0] = jnp.where(first, 0.0, 0.5 * (low + diff[0]))
    gz[planes] = jnp.where(last, 0.0, 0.5 * (diff[planes - 1] + high))
    coefficients(0, diff[0], low, diff[1], labels[0], flow[0])
    coefficients(planes - 1, diff[planes - 1], diff[planes - 2], high,
                 labels[planes - 1], flow[planes - 1])
    coefficients(below, halo[0][1], halo[0][0], diff[0], lab_h[0, 1], flow_h[0])
    coefficients(above, halo[1][0], diff[planes - 1], halo[1][1], lab_h[1, 0], flow_h[1])
    far = (0.5 * (halo[0][0] + halo[0][1]), 0.5 * (halo[1][0] + halo[1][1]))
    gz[planes + 1] = far[0]
    gz[planes + 2] = far[1]
    for slot, k in enumerate(ends):
        for p in range(pairs):
            d0[k, p] = src[slot, p] * inv[k, p] * (1.0 / CENTRE)
    for k in inner:
        for p in range(pairs):
            advance(k, p, inside(d0, k, p))
    settle_halo(sent_src)
    for side, k in enumerate((below, above)):
        for p in range(pairs):
            d0[k, p] = src_h[side, p] * inv[k, p] * (1.0 / CENTRE)
    for k in ends:
        for p in range(pairs):
            advance(k, p, inside(d0, k, p))
    copy = loads[2]
    copy.wait()
    order = inner + ends
    for slot, k in enumerate(inner):
        part[slot] = finish(k)
    sums = scatter(0, 0, len(inner))
    settle_halo(sent_far)
    for p in range(pairs):
        advance(below, p, gather(
            d0, below, p, gz[planes + 1], gz[0], d0_far[0, p], d0[0, p]))
        advance(above, p, gather(
            d0, above, p, gz[planes], gz[planes + 2], d0[planes - 1, p], d0_far[1, p]))
    for slot, k in enumerate(ends):
        part[len(inner) + slot] = finish(k)
    sums += scatter(1, len(inner), planes)
    for copy in sums:
        copy.wait()
    own = pl.ds(pl.multiple_of(me * rows_out, rows_out), rows_out)
    for slot, k in enumerate(order):
        total = part[slot, own, :]
        for step in range(groups - 1):
            total = total + recv[step, slot]
        out[k] = total


def body(
    forward, detectors, residuals, delay_index, labels, blood_flow,
    diff_table, absorb_table, delay_tau, delay_weight,
):
    groups = lax.axis_size("src")
    depths = lax.axis_size("depth")
    pairs, planes = forward.shape[0], forward.shape[1]
    count = detectors.shape[0]
    vmem = pl.BlockSpec(memory_space=pltpu.VMEM)
    hbm = pl.BlockSpec(memory_space=pl.ANY)
    smem = pl.BlockSpec(memory_space=pltpu.SMEM)
    dma = pltpu.SemaphoreType.DMA
    plane = lambda *lead: pltpu.VMEM(lead + (N, N), F32)
    return pl.pallas_call(
        functools.partial(kernel, groups, depths),
        out_shape=jax.ShapeDtypeStruct((planes, N // groups, N), F32),
        in_specs=[hbm, vmem, vmem, hbm, hbm] + [smem] * 5,
        out_specs=vmem,
        scratch_shapes=[
            pltpu.VMEM((pairs, planes, N, N), BF16),
            pltpu.VMEM((planes, N, N), jnp.int32),
            plane(planes),
            pltpu.VMEM((2 * pairs * N, count), BF16),
            pltpu.VMEM((2 * N, 2 * pairs * N), F32),
            pltpu.VMEM((2, 2, N, N), jnp.int32),
            plane(2),
            plane(planes),
            plane(planes + 2, pairs),
            plane(planes + 2),
            plane(planes + 2),
            plane(planes + 3),
            plane(2, pairs),
            plane(2, pairs),
            plane(planes + 2, pairs),
            plane(2, pairs),
            plane(planes + 2, pairs),
            plane(planes, pairs),
            plane(planes),
            pltpu.VMEM((groups - 1, planes, N // groups, N), F32),
            dma((3,)), dma((2,)), dma((2,)), dma((2,)), dma((2,)), dma((2,)), dma((2,)),
            dma((2,)), dma((2,)), dma((4,)), dma((4,)),
            dma((2, groups - 1)), dma((2, groups - 1)),
        ],
        compiler_params=pltpu.CompilerParams(collective_id=0, has_side_effects=True),
        name="flow_gradient",
    )(
        forward, detectors.reshape(1, count), residuals, labels, blood_flow,
        delay_index, diff_table, absorb_table, delay_tau, delay_weight,
    )


def solution(mesh):
    placed = (
        P("src", "depth", None, None),
        P("depth"),
        P("src", "depth"),
        P("src"),
        P("depth", None, None),
        P("depth", None, None),
        P(),
        P(),
        P(),
        P(),
    )
    return jax.shard_map(
        body, mesh=mesh, in_specs=placed, out_specs=P("depth", "src", None), check_vma=False
    )
```

```python
import functools

import jax
import jax.numpy as jnp
from jax import lax
from jax.experimental import pallas as pl
from jax.experimental.pallas import tpu as pltpu
from jax.sharding import PartitionSpec as P

SPECTRUM_LOW = 0.1
SPECTRUM_HIGH = 2.0
CENTRE = 0.5 * (SPECTRUM_HIGH + SPECTRUM_LOW)
HALF = 0.5 * (SPECTRUM_HIGH - SPECTRUM_LOW)
SIGMA = CENTRE / HALF
RHO0 = 1.0 / SIGMA
RHO1 = 1.0 / (2.0 * SIGMA - RHO0)
RHO2 = 1.0 / (2.0 * SIGMA - RHO1)

N = 128
CHUNK = 4096
MESH = pl.DeviceIdType.MESH
F32 = jnp.float32
BF16 = jnp.bfloat16


def lookup(table, labels, count):
    value = jnp.zeros(labels.shape, F32)
    for entry in range(count):
        value = jnp.where(labels == entry, table[entry], value)
    return value


def kernel(
    groups, depths,
    fwd_in, det, res, labels_in, flow_in, index, dtab, atab, tau, wgt,
    out,
    fwd, labels, flow, rt, acc, lab_h, flow_h, diff, inv, gx, gy, gz,
    src, src_h, d0, d0_far, d1, q1, part, recv,
    in_s, lab_s, lab_r, flow_s, flow_r, src_s, src_r, far_s, far_r, pass_s, pass_r,
    rs_s, rs_r,
):
    me = lax.axis_index("src")
    z = lax.axis_index("depth")
    up = jnp.minimum(z + 1, depths - 1)
    down = jnp.maximum(z - 1, 0)
    first = z == 0
    last = z == depths - 1
    pairs, planes = fwd.shape[0], fwd.shape[1]
    count = det.shape[1]

    barrier = pltpu.get_barrier_semaphore()
    inside_low = z > 0
    inside_high = z < depths - 1
    for has, side in ((inside_high, up), (inside_low, down)):
        @pl.when(has)
        def _(side=side):
            pl.semaphore_signal(barrier, inc=1, device_id={"depth": side}, device_id_type=MESH)
    for step in range(1, groups):
        peer = lax.rem(me + step, groups)
        pl.semaphore_signal(barrier, inc=1, device_id={"src": peer}, device_id_type=MESH)
    loads = [
        pltpu.make_async_copy(labels_in, labels, in_s.at[0]),
        pltpu.make_async_copy(flow_in, flow, in_s.at[1]),
        pltpu.make_async_copy(fwd_in, fwd, in_s.at[2]),
    ]
    for copy in loads:
        copy.start()

    def shift(to_up, from_below, to_down, from_above, send, receive):
        pair = (
            pltpu.make_async_remote_copy(
                to_up, from_below, send.at[0], receive.at[0],
                device_id={"depth": up}, device_id_type=MESH),
            pltpu.make_async_remote_copy(
                to_down, from_above, send.at[1], receive.at[1],
                device_id={"depth": down}, device_id_type=MESH),
        )
        return pair

    def launch(pair):
        pl.when(inside_high)(pair[0].start)
        pl.when(inside_low)(pair[1].start)
        return pair

    def settle_halo(pair):
        @pl.when(inside_high)
        def _():
            pair[0].wait_send()
            pair[1].wait_recv()

        @pl.when(inside_low)
        def _():
            pair[0].wait_recv()
            pair[1].wait_send()

    for has, side in ((first, 0), (last, 1)):
        @pl.when(has)
        def _(side=side):
            lab_h[side] = jnp.zeros(lab_h.shape[1:], jnp.int32)
            flow_h[side] = jnp.ones(flow_h.shape[1:], F32)
            src_h[side] = jnp.zeros(src_h.shape[1:], F32)
            d0_far[side] = jnp.zeros(d0_far.shape[1:], F32)

    row16 = lax.broadcasted_iota(jnp.int32, (16, CHUNK), 0).astype(F32)
    ids = [(row16 + 16.0 * b).astype(BF16) for b in range(N // 16)]
    zero = jnp.zeros((16, CHUNK), BF16)
    one = jnp.ones((16, CHUNK), BF16)

    def spread(row):
        return jnp.broadcast_to(row, (16, CHUNK)).astype(BF16)

    def rows_of(detectors, plane):
        mine = spread(((detectors >> 7) - plane * N).astype(F32))
        return [jnp.where(mine == ids[b], one, zero) for b in range(N // 16)]

    def select(chunk, wanted, fresh):
        start = pl.multiple_of(chunk * CHUNK, CHUNK)
        detectors = det[:, pl.ds(start, CHUNK)]
        if fresh:
            column = spread((detectors & (N - 1)).astype(F32))
            weights = []
            for p in range(pairs):
                value = res[p:p + 1, pl.ds(start, CHUNK)]
                head = value.astype(BF16).astype(F32)
                weights.append((p, spread(head)))
                weights.append((pairs + p, spread(value - head)))
            for b in range(N // 16):
                hit = column == ids[b]
                for slot, weight in weights:
                    rt[slot * N + 16 * b:slot * N + 16 * b + 16, pl.ds(start, CHUNK)] = (
                        jnp.where(hit, weight, zero))
        rows = []
        for plane in wanted:
            rows += rows_of(detectors, plane)
        onehot = jnp.concatenate(rows, axis=0)
        acc[...] += lax.dot_general(
            onehot, rt[:, pl.ds(start, CHUNK)], (((1,), (1,)), ((), ())),
            preferred_element_type=F32)

    def run(wanted, fresh, at, act):
        def step(chunk, carry):
            pl.when(chunk == at)(act)
            select(chunk, wanted, fresh)
            return carry
        lax.fori_loop(0, count // CHUNK, step, 0)

    def source(slot, p):
        rows = slice(slot * N, (slot + 1) * N)
        return acc[rows, p * N:(p + 1) * N] + acc[rows, (pairs + p) * N:(pairs + p + 1) * N]

    ends = (0, planes - 1)
    inner = tuple(range(1, planes - 1))
    below, above = planes, planes + 1

    half = N // 2
    mine = pl.ds(pl.multiple_of(lax.rem(me, 2) * half, half), half)
    twin = me + 1 - 2 * lax.rem(me, 2)
    sent_labels = shift(
        labels.at[planes - 2:planes, mine], lab_h.at[0, :, mine],
        labels.at[0:2, mine], lab_h.at[1, :, mine], lab_s, lab_r)
    sent_flow = shift(
        flow.at[planes - 1, mine], flow_h.at[0, mine],
        flow.at[0, mine], flow_h.at[1, mine], flow_s, flow_r)

    def enter():
        pl.semaphore_wait(
            barrier, groups - 1 + jnp.minimum(z, 1) + jnp.minimum(depths - 1 - z, 1))
        for copy in loads[:2]:
            copy.wait()
        launch(sent_labels)
        launch(sent_flow)

    acc[...] = jnp.zeros_like(acc)
    run(ends, True, 1, enter)
    for slot in range(2):
        for p in range(pairs):
            src[slot, p] = source(slot, p)
    sent_src = launch(shift(
        src.at[1], src_h.at[0], src.at[0], src_h.at[1], src_s, src_r))

    lane = lax.broadcasted_iota(jnp.int32, (N, N), 1)
    row = lax.broadcasted_iota(jnp.int32, (N, N), 0)
    taus = [tau[index[p]] for p in range(pairs)]

    def coefficients(k, here, under, over, label, stream):
        right = jnp.where(lane < N - 1, pltpu.roll(here, N - 1, 1), 0.0)
        left = jnp.where(lane > 0, pltpu.roll(here, 1, 1), 0.0)
        south = jnp.where(row < N - 1, pltpu.roll(here, N - 1, 0), 0.0)
        north = jnp.where(row > 0, pltpu.roll(here, 1, 0), 0.0)
        gx[k] = jnp.where(lane < N - 1, 0.5 * (here + right), 0.0)
        gy[k] = jnp.where(row < N - 1, 0.5 * (here + south), 0.0)
        faces = 3.0 * here + 0.5 * ((left + right) + (north + south) + (under + over))
        base = lookup(atab, label, atab.shape[0]) + faces
        for p in range(pairs):
            inv[k, p] = 1.0 / (base + taus[p] * stream)

    def gather(field, k, p, lower, upper, under, over):
        here = field[k, p]
        fx, fy = gx[k], gy[k]
        total = lower * under + upper * over
        total += fx * pltpu.roll(here, N - 1, 1) + pltpu.roll(fx * here, 1, 1)
        total += fy * pltpu.roll(here, N - 1, 0) + pltpu.roll(fy * here, 1, 0)
        return total

    def inside(field, k, p):
        under = field[below if k == 0 else k - 1, p]
        over = field[above if k == planes - 1 else k + 1, p]
        return gather(field, k, p, gz[k], gz[k + 1], under, over)

    def advance(k, p, shared):
        old = d0[k, p]
        ratio = (CENTRE - 1.0) * old + inv[k, p] * shared
        d1[k, p] = (RHO1 * RHO0) * old + (2.0 * RHO1 / HALF) * ratio
        if k < planes:
            q1[k, p] = ratio

    def finish(k):
        total = None
        for p in range(pairs):
            old = d1[k, p]
            ratio = q1[k, p] - old + inv[k, p] * inside(d1, k, p)
            field = d0[k, p] + (1.0 + RHO2 * RHO1) * old + (2.0 * RHO2 / HALF) * ratio
            coef = -(wgt[index[p]] * taus[p])
            term = coef * fwd[p, k].astype(F32) * field
            total = term if total is None else total + term
        return total

    rows_out = N // groups

    def scatter(phase, low, high):
        sent = []
        for step in range(1, groups):
            peer = lax.rem(me + step, groups)
            rows = pl.ds(pl.multiple_of(peer * rows_out, rows_out), rows_out)
            copy = pltpu.make_async_remote_copy(
                part.at[low:high, rows, :], recv.at[step - 1, low:high],
                rs_s.at[phase, step - 1], rs_r.at[phase, step - 1],
                device_id={"src": peer}, device_id_type=MESH)
            copy.start()
            sent.append(copy)
        return sent

    for k in range(planes):
        diff[k] = lookup(dtab, labels[k], dtab.shape[0])
    for k in range(1, planes):
        gz[k] = 0.5 * (diff[k - 1] + diff[k])
    for k in inner:
        coefficients(k, diff[k], diff[k - 1], diff[k + 1], labels[k], flow[k])

    acc[...] = jnp.zeros_like(acc)
    relays = [
        pltpu.make_async_remote_copy(
            ref, ref, pass_s.at[slot], pass_r.at[slot],
            device_id={"src": twin}, device_id_type=MESH)
        for slot, ref in enumerate((
            lab_h.at[0, :, mine], flow_h.at[0, mine], lab_h.at[1, :, mine], flow_h.at[1, mine]))
    ]

    def each_relay(act):
        for has, pair in ((inside_low, relays[:2]), (inside_high, relays[2:])):
            @pl.when(has)
            def _(pair=pair):
                for copy in pair:
                    act(copy)

    def hand_over():
        settle_halo(sent_labels)
        settle_halo(sent_flow)
        each_relay(lambda copy: copy.start())

    run(inner, False, 2, hand_over)
    for slot, k in enumerate(inner):
        for p in range(pairs):
            d0[k, p] = source(slot, p) * inv[k, p] * (1.0 / CENTRE)
    sent_far = launch(shift(
        d0.at[planes - 2], d0_far.at[0], d0.at[1], d0_far.at[1], far_s, far_r))

    each_relay(lambda copy: copy.wait())
    halo = [[lookup(dtab, lab_h[s, i], dtab.shape[0]) for i in range(2)] for s in range(2)]
    low = jnp.where(first, 0.0, halo[0][1])
    high = jnp.where(last, 0.0, halo[1][0])
    gz[0] = jnp.where(first, 0.0, 0.5 * (low + diff[0]))
    gz[planes] = jnp.where(last, 0.0, 0.5 * (diff[planes - 1] + high))
    coefficients(0, diff[0], low, diff[1], labels[0], flow[0])
    coefficients(planes - 1, diff[planes - 1], diff[planes - 2], high,
                 labels[planes - 1], flow[planes - 1])
    coefficients(below, halo[0][1], halo[0][0], diff[0], lab_h[0, 1], flow_h[0])
    coefficients(above, halo[1][0], diff[planes - 1], halo[1][1], lab_h[1, 0], flow_h[1])
    far = (0.5 * (halo[0][0] + halo[0][1]), 0.5 * (halo[1][0] + halo[1][1]))
    gz[planes + 1] = far[0]
    gz[planes + 2] = far[1]
    for slot, k in enumerate(ends):
        for p in range(pairs):
            d0[k, p] = src[slot, p] * inv[k, p] * (1.0 / CENTRE)
    for k in inner:
        for p in range(pairs):
            advance(k, p, inside(d0, k, p))
    settle_halo(sent_src)
    for side, k in enumerate((below, above)):
        for p in range(pairs):
            d0[k, p] = src_h[side, p] * inv[k, p] * (1.0 / CENTRE)
    for k in ends:
        for p in range(pairs):
            advance(k, p, inside(d0, k, p))
    copy = loads[2]
    copy.wait()
    order = inner + ends
    for slot, k in enumerate(inner):
        part[slot] = finish(k)
    sums = scatter(0, 0, len(inner))
    settle_halo(sent_far)
    for p in range(pairs):
        advance(below, p, gather(
            d0, below, p, gz[planes + 1], gz[0], d0_far[0, p], d0[0, p]))
        advance(above, p, gather(
            d0, above, p, gz[planes], gz[planes + 2], d0[planes - 1, p], d0_far[1, p]))
    for slot, k in enumerate(ends):
        part[len(inner) + slot] = finish(k)
    sums += scatter(1, len(inner), planes)
    for copy in sums:
        copy.wait()
    own = pl.ds(pl.multiple_of(me * rows_out, rows_out), rows_out)
    for slot, k in enumerate(order):
        total = part[slot, own, :]
        for step in range(groups - 1):
            total = total + recv[step, slot]
        out[k] = total


def body(
    forward, detectors, residuals, delay_index, labels, blood_flow,
    diff_table, absorb_table, delay_tau, delay_weight,
):
    groups = lax.axis_size("src")
    depths = lax.axis_size("depth")
    pairs, planes = forward.shape[0], forward.shape[1]
    count = detectors.shape[0]
    vmem = pl.BlockSpec(memory_space=pltpu.VMEM)
    hbm = pl.BlockSpec(memory_space=pl.ANY)
    smem = pl.BlockSpec(memory_space=pltpu.SMEM)
    dma = pltpu.SemaphoreType.DMA
    plane = lambda *lead: pltpu.VMEM(lead + (N, N), F32)
    return pl.pallas_call(
        functools.partial(kernel, groups, depths),
        out_shape=jax.ShapeDtypeStruct((planes, N // groups, N), F32),
        in_specs=[hbm, vmem, vmem, hbm, hbm] + [smem] * 5,
        out_specs=vmem,
        scratch_shapes=[
            pltpu.VMEM((pairs, planes, N, N), BF16),
            pltpu.VMEM((planes, N, N), jnp.int32),
            plane(planes),
            pltpu.VMEM((2 * pairs * N, count), BF16),
            pltpu.VMEM((2 * N, 2 * pairs * N), F32),
            pltpu.VMEM((2, 2, N, N), jnp.int32),
            plane(2),
            plane(planes),
            plane(planes + 2, pairs),
            plane(planes + 2),
            plane(planes + 2),
            plane(planes + 3),
            plane(2, pairs),
            plane(2, pairs),
            plane(planes + 2, pairs),
            plane(2, pairs),
            plane(planes + 2, pairs),
            plane(planes, pairs),
            plane(planes),
            pltpu.VMEM((groups - 1, planes, N // groups, N), F32),
            dma((3,)), dma((2,)), dma((2,)), dma((2,)), dma((2,)), dma((2,)), dma((2,)),
            dma((2,)), dma((2,)), dma((4,)), dma((4,)),
            dma((2, groups - 1)), dma((2, groups - 1)),
        ],
        compiler_params=pltpu.CompilerParams(collective_id=0, has_side_effects=True),
        name="flow_gradient",
    )(
        forward, detectors.reshape(1, count), residuals, labels, blood_flow,
        delay_index, diff_table, absorb_table, delay_tau, delay_weight,
    )


def solution(mesh):
    placed = (
        P("src", "depth", None, None),
        P("depth"),
        P("src", "depth"),
        P("src"),
        P("depth", None, None),
        P("depth", None, None),
        P(),
        P(),
        P(),
        P(),
    )
    return jax.shard_map(
        body, mesh=mesh, in_specs=placed, out_specs=P("depth", "src", None), check_vma=False
    )
```

```python
import functools

import jax
import jax.numpy as jnp
from jax import lax
from jax.experimental import pallas as pl
from jax.experimental.pallas import tpu as pltpu
from jax.sharding import PartitionSpec as P

SPECTRUM_LOW = 0.1
SPECTRUM_HIGH = 2.0
CENTRE = 0.5 * (SPECTRUM_HIGH + SPECTRUM_LOW)
HALF = 0.5 * (SPECTRUM_HIGH - SPECTRUM_LOW)
SIGMA = CENTRE / HALF
RHO0 = 1.0 / SIGMA
RHO1 = 1.0 / (2.0 * SIGMA - RHO0)
RHO2 = 1.0 / (2.0 * SIGMA - RHO1)

N = 128
CHUNK = 4096
MESH = pl.DeviceIdType.MESH
F32 = jnp.float32
BF16 = jnp.bfloat16


def lookup(table, labels, count):
    value = jnp.zeros(labels.shape, F32)
    for entry in range(count):
        value = jnp.where(labels == entry, table[entry], value)
    return value


def kernel(
    groups, depths,
    fwd_in, det, res, labels_in, flow_in, index, dtab, atab, tau, wgt,
    out,
    fwd, labels, flow, rt, acc, lab_h, flow_h, diff, inv, gx, gy, gz,
    src, src_h, d0, d0_far, d1, q1, part, recv,
    in_s, lab_s, lab_r, flow_s, flow_r, src_s, src_r, far_s, far_r, pass_s, pass_r,
    rs_s, rs_r,
):
    me = lax.axis_index("src")
    z = lax.axis_index("depth")
    up = jnp.minimum(z + 1, depths - 1)
    down = jnp.maximum(z - 1, 0)
    first = z == 0
    last = z == depths - 1
    pairs, planes = fwd.shape[0], fwd.shape[1]
    count = det.shape[1]

    barrier = pltpu.get_barrier_semaphore()
    inside_low = z > 0
    inside_high = z < depths - 1
    for has, side in ((inside_high, up), (inside_low, down)):
        @pl.when(has)
        def _(side=side):
            pl.semaphore_signal(barrier, inc=1, device_id={"depth": side}, device_id_type=MESH)
    for step in range(1, groups):
        peer = lax.rem(me + step, groups)
        pl.semaphore_signal(barrier, inc=1, device_id={"src": peer}, device_id_type=MESH)
    loads = [
        pltpu.make_async_copy(labels_in, labels, in_s.at[0]),
        pltpu.make_async_copy(flow_in, flow, in_s.at[1]),
        pltpu.make_async_copy(fwd_in, fwd, in_s.at[2]),
    ]
    for copy in loads:
        copy.start()

    def shift(to_up, from_below, to_down, from_above, send, receive):
        pair = (
            pltpu.make_async_remote_copy(
                to_up, from_below, send.at[0], receive.at[0],
                device_id={"depth": up}, device_id_type=MESH),
            pltpu.make_async_remote_copy(
                to_down, from_above, send.at[1], receive.at[1],
                device_id={"depth": down}, device_id_type=MESH),
        )
        return pair

    def launch(pair):
        pl.when(inside_high)(pair[0].start)
        pl.when(inside_low)(pair[1].start)
        return pair

    def settle_halo(pair):
        @pl.when(inside_high)
        def _():
            pair[0].wait_send()
            pair[1].wait_recv()

        @pl.when(inside_low)
        def _():
            pair[0].wait_recv()
            pair[1].wait_send()

    for has, side in ((first, 0), (last, 1)):
        @pl.when(has)
        def _(side=side):
            lab_h[side] = jnp.zeros(lab_h.shape[1:], jnp.int32)
            flow_h[side] = jnp.ones(flow_h.shape[1:], F32)
            src_h[side] = jnp.zeros(src_h.shape[1:], F32)
            d0_far[side] = jnp.zeros(d0_far.shape[1:], F32)

    row16 = lax.broadcasted_iota(jnp.int32, (16, CHUNK), 0).astype(F32)
    ids = [(row16 + 16.0 * b).astype(BF16) for b in range(N // 16)]
    zero = jnp.zeros((16, CHUNK), BF16)
    one = jnp.ones((16, CHUNK), BF16)

    def spread(row):
        return jnp.broadcast_to(row, (16, CHUNK)).astype(BF16)

    def rows_of(detectors, plane):
        mine = spread(((detectors >> 7) - plane * N).astype(F32))
        return [jnp.where(mine == ids[b], one, zero) for b in range(N // 16)]

    def select(chunk, wanted, fresh):
        start = pl.multiple_of(chunk * CHUNK, CHUNK)
        detectors = det[:, pl.ds(start, CHUNK)]
        if fresh:
            column = spread((detectors & (N - 1)).astype(F32))
            weights = []
            for p in range(pairs):
                value = res[p:p + 1, pl.ds(start, CHUNK)]
                head = value.astype(BF16).astype(F32)
                weights.append((p, spread(head)))
                weights.append((pairs + p, spread(value - head)))
            for b in range(N // 16):
                hit = column == ids[b]
                for slot, weight in weights:
                    rt[slot * N + 16 * b:slot * N + 16 * b + 16, pl.ds(start, CHUNK)] = (
                        jnp.where(hit, weight, zero))
        rows = []
        for plane in wanted:
            rows += rows_of(detectors, plane)
        onehot = jnp.concatenate(rows, axis=0)
        acc[...] += lax.dot_general(
            onehot, rt[:, pl.ds(start, CHUNK)], (((1,), (1,)), ((), ())),
            preferred_element_type=F32)

    def run(wanted, fresh, at, act):
        def step(chunk, carry):
            pl.when(chunk == at)(act)
            select(chunk, wanted, fresh)
            return carry
        lax.fori_loop(0, count // CHUNK, step, 0)

    def source(slot, p):
        rows = slice(slot * N, (slot + 1) * N)
        return acc[rows, p * N:(p + 1) * N] + acc[rows, (pairs + p) * N:(pairs + p + 1) * N]

    ends = (0, planes - 1)
    inner = tuple(range(1, planes - 1))
    below, above = planes, planes + 1

    half = N // 2
    mine = pl.ds(pl.multiple_of(lax.rem(me, 2) * half, half), half)
    twin = me + 1 - 2 * lax.rem(me, 2)
    sent_labels = shift(
        labels.at[planes - 2:planes, mine], lab_h.at[0, :, mine],
        labels.at[0:2, mine], lab_h.at[1, :, mine], lab_s, lab_r)
    sent_flow = shift(
        flow.at[planes - 1, mine], flow_h.at[0, mine],
        flow.at[0, mine], flow_h.at[1, mine], flow_s, flow_r)

    def enter():
        pl.semaphore_wait(
            barrier, groups - 1 + jnp.minimum(z, 1) + jnp.minimum(depths - 1 - z, 1))
        for copy in loads[:2]:
            copy.wait()
        launch(sent_labels)
        launch(sent_flow)

    acc[...] = jnp.zeros_like(acc)
    run(ends, True, 1, enter)
    for slot in range(2):
        for p in range(pairs):
            src[slot, p] = source(slot, p)
    sent_src = launch(shift(
        src.at[1], src_h.at[0], src.at[0], src_h.at[1], src_s, src_r))

    lane = lax.broadcasted_iota(jnp.int32, (N, N), 1)
    row = lax.broadcasted_iota(jnp.int32, (N, N), 0)
    taus = [tau[index[p]] for p in range(pairs)]

    def coefficients(k, here, under, over, label, stream):
        right = jnp.where(lane < N - 1, pltpu.roll(here, N - 1, 1), 0.0)
        left = jnp.where(lane > 0, pltpu.roll(here, 1, 1), 0.0)
        south = jnp.where(row < N - 1, pltpu.roll(here, N - 1, 0), 0.0)
        north = jnp.where(row > 0, pltpu.roll(here, 1, 0), 0.0)
        gx[k] = jnp.where(lane < N - 1, 0.5 * (here + right), 0.0)
        gy[k] = jnp.where(row < N - 1, 0.5 * (here + south), 0.0)
        faces = 3.0 * here + 0.5 * ((left + right) + (north + south) + (under + over))
        base = lookup(atab, label, atab.shape[0]) + faces
        for p in range(pairs):
            inv[k, p] = 1.0 / (base + taus[p] * stream)

    def gather(field, k, p, lower, upper, under, over):
        here = field[k, p]
        fx, fy = gx[k], gy[k]
        total = lower * under + upper * over
        total += fx * pltpu.roll(here, N - 1, 1) + pltpu.roll(fx * here, 1, 1)
        total += fy * pltpu.roll(here, N - 1, 0) + pltpu.roll(fy * here, 1, 0)
        return total

    def inside(field, k, p):
        under = field[below if k == 0 else k - 1, p]
        over = field[above if k == planes - 1 else k + 1, p]
        return gather(field, k, p, gz[k], gz[k + 1], under, over)

    def advance(k, p, shared):
        old = d0[k, p]
        ratio = (CENTRE - 1.0) * old + inv[k, p] * shared
        d1[k, p] = (RHO1 * RHO0) * old + (2.0 * RHO1 / HALF) * ratio
        if k < planes:
            q1[k, p] = ratio

    def finish(k):
        total = None
        for p in range(pairs):
            old = d1[k, p]
            ratio = q1[k, p] - old + inv[k, p] * inside(d1, k, p)
            field = d0[k, p] + (1.0 + RHO2 * RHO1) * old + (2.0 * RHO2 / HALF) * ratio
            coef = -(wgt[index[p]] * taus[p])
            term = coef * fwd[p, k].astype(F32) * field
            total = term if total is None else total + term
        return total

    rows_out = N // groups

    def scatter(phase, low, high):
        sent = []
        for step in range(1, groups):
            peer = lax.rem(me + step, groups)
            rows = pl.ds(pl.multiple_of(peer * rows_out, rows_out), rows_out)
            copy = pltpu.make_async_remote_copy(
                part.at[low:high, rows, :], recv.at[step - 1, low:high],
                rs_s.at[phase, step - 1], rs_r.at[phase, step - 1],
                device_id={"src": peer}, device_id_type=MESH)
            copy.start()
            sent.append(copy)
        return sent

    for k in range(planes):
        diff[k] = lookup(dtab, labels[k], dtab.shape[0])
    for k in range(1, planes):
        gz[k] = 0.5 * (diff[k - 1] + diff[k])
    for k in inner:
        coefficients(k, diff[k], diff[k - 1], diff[k + 1], labels[k], flow[k])

    acc[...] = jnp.zeros_like(acc)
    relays = [
        pltpu.make_async_remote_copy(
            ref, ref, pass_s.at[slot], pass_r.at[slot],
            device_id={"src": twin}, device_id_type=MESH)
        for slot, ref in enumerate((
            lab_h.at[0, :, mine], flow_h.at[0, mine], lab_h.at[1, :, mine], flow_h.at[1, mine]))
    ]

    def each_relay(act):
        for has, pair in ((inside_low, relays[:2]), (inside_high, relays[2:])):
            @pl.when(has)
            def _(pair=pair):
                for copy in pair:
                    act(copy)

    def hand_over():
        settle_halo(sent_labels)
        settle_halo(sent_flow)
        each_relay(lambda copy: copy.start())

    run(inner, False, 2, hand_over)
    for slot, k in enumerate(inner):
        for p in range(pairs):
            d0[k, p] = source(slot, p) * inv[k, p] * (1.0 / CENTRE)
    sent_far = launch(shift(
        d0.at[planes - 2], d0_far.at[0], d0.at[1], d0_far.at[1], far_s, far_r))

    each_relay(lambda copy: copy.wait())
    halo = [[lookup(dtab, lab_h[s, i], dtab.shape[0]) for i in range(2)] for s in range(2)]
    low = jnp.where(first, 0.0, halo[0][1])
    high = jnp.where(last, 0.0, halo[1][0])
    gz[0] = jnp.where(first, 0.0, 0.5 * (low + diff[0]))
    gz[planes] = jnp.where(last, 0.0, 0.5 * (diff[planes - 1] + high))
    coefficients(0, diff[0], low, diff[1], labels[0], flow[0])
    coefficients(planes - 1, diff[planes - 1], diff[planes - 2], high,
                 labels[planes - 1], flow[planes - 1])
    coefficients(below, halo[0][1], halo[0][0], diff[0], lab_h[0, 1], flow_h[0])
    coefficients(above, halo[1][0], diff[planes - 1], halo[1][1], lab_h[1, 0], flow_h[1])
    far = (0.5 * (halo[0][0] + halo[0][1]), 0.5 * (halo[1][0] + halo[1][1]))
    gz[planes + 1] = far[0]
    gz[planes + 2] = far[1]
    for slot, k in enumerate(ends):
        for p in range(pairs):
            d0[k, p] = src[slot, p] * inv[k, p] * (1.0 / CENTRE)
    for k in inner:
        for p in range(pairs):
            advance(k, p, inside(d0, k, p))
    settle_halo(sent_src)
    for side, k in enumerate((below, above)):
        for p in range(pairs):
            d0[k, p] = src_h[side, p] * inv[k, p] * (1.0 / CENTRE)
    for k in ends:
        for p in range(pairs):
            advance(k, p, inside(d0, k, p))
    copy = loads[2]
    copy.wait()
    order = inner + ends
    for slot, k in enumerate(inner):
        part[slot] = finish(k)
    sums = scatter(0, 0, len(inner))
    blank = jnp.zeros((N, N), F32)
    for p in range(pairs):
        advance(below, p, gather(d0, below, p, blank, gz[0], blank, d0[0, p]))
        advance(above, p, gather(d0, above, p, gz[planes], blank, d0[planes - 1, p], blank))
    sides = ((0, below, gz[planes + 1] * gz[0]), (planes - 1, above, gz[planes + 2] * gz[planes]))
    for slot, (k, beyond, faces) in enumerate(sides):
        part[len(inner) + slot] = finish(k)
        for p in range(pairs):
            coef = -(wgt[index[p]] * taus[p]) * (4.0 * RHO1 * RHO2 / HALF / HALF)
            src[slot, p] = coef * fwd[p, k].astype(F32) * faces * (inv[k, p] * inv[beyond, p])
    settle_halo(sent_far)
    for slot in range(2):
        total = part[len(inner) + slot]
        for p in range(pairs):
            total = total + src[slot, p] * d0_far[slot, p]
        part[len(inner) + slot] = total
    sums += scatter(1, len(inner), planes)
    for copy in sums:
        copy.wait()
    own = pl.ds(pl.multiple_of(me * rows_out, rows_out), rows_out)
    for slot, k in enumerate(order):
        total = part[slot, own, :]
        for step in range(groups - 1):
            total = total + recv[step, slot]
        out[k] = total


def body(
    forward, detectors, residuals, delay_index, labels, blood_flow,
    diff_table, absorb_table, delay_tau, delay_weight,
):
    groups = lax.axis_size("src")
    depths = lax.axis_size("depth")
    pairs, planes = forward.shape[0], forward.shape[1]
    count = detectors.shape[0]
    vmem = pl.BlockSpec(memory_space=pltpu.VMEM)
    hbm = pl.BlockSpec(memory_space=pl.ANY)
    smem = pl.BlockSpec(memory_space=pltpu.SMEM)
    dma = pltpu.SemaphoreType.DMA
    plane = lambda *lead: pltpu.VMEM(lead + (N, N), F32)
    return pl.pallas_call(
        functools.partial(kernel, groups, depths),
        out_shape=jax.ShapeDtypeStruct((planes, N // groups, N), F32),
        in_specs=[hbm, vmem, vmem, hbm, hbm] + [smem] * 5,
        out_specs=vmem,
        scratch_shapes=[
            pltpu.VMEM((pairs, planes, N, N), BF16),
            pltpu.VMEM((planes, N, N), jnp.int32),
            plane(planes),
            pltpu.VMEM((2 * pairs * N, count), BF16),
            pltpu.VMEM((2 * N, 2 * pairs * N), F32),
            pltpu.VMEM((2, 2, N, N), jnp.int32),
            plane(2),
            plane(planes),
            plane(planes + 2, pairs),
            plane(planes + 2),
            plane(planes + 2),
            plane(planes + 3),
            plane(2, pairs),
            plane(2, pairs),
            plane(planes + 2, pairs),
            plane(2, pairs),
            plane(planes + 2, pairs),
            plane(planes, pairs),
            plane(planes),
            pltpu.VMEM((groups - 1, planes, N // groups, N), F32),
            dma((3,)), dma((2,)), dma((2,)), dma((2,)), dma((2,)), dma((2,)), dma((2,)),
            dma((2,)), dma((2,)), dma((4,)), dma((4,)),
            dma((2, groups - 1)), dma((2, groups - 1)),
        ],
        compiler_params=pltpu.CompilerParams(collective_id=0, has_side_effects=True),
        name="flow_gradient",
    )(
        forward, detectors.reshape(1, count), residuals, labels, blood_flow,
        delay_index, diff_table, absorb_table, delay_tau, delay_weight,
    )


def solution(mesh):
    placed = (
        P("src", "depth", None, None),
        P("depth"),
        P("src", "depth"),
        P("src"),
        P("depth", None, None),
        P("depth", None, None),
        P(),
        P(),
        P(),
        P(),
    )
    return jax.shard_map(
        body, mesh=mesh, in_specs=placed, out_specs=P("depth", "src", None), check_vma=False
    )
```
